128 devices in a mesh: seq: 8 (over y, x_hi), hid: 16 (over z, x_lo, core).
Axes of the slice: x: 4 (x_hi: 2, x_lo: 2; x = x_hi * 2 + x_lo), y: 4, z: 4, core: 2. Of those that a mesh axis runs over, the one named last changes fastest.
Arguments:
- tokens: bfloat16 [5120, 5120], P('seq', 'hid'), may hold values from -18 to 18
- clip_id: int32 [5120], P('seq'), may hold values from 0 to 7, never falling along the last dimension, each value on 1 to 3200 neighbouring positions
- clip_step: int32 [8], replicated, may hold values from 0 to 31
- mod_table: float32 [32, 6, 5120], replicated, may hold values from -3 to 3
- w_query: bfloat16 [5120, 4096], P(None, 'hid'), may hold values from -3 to 3
- w_key: bfloat16 [5120, 4096], P(None, 'hid'), may hold values from -3 to 3
- w_value: bfloat16 [5120, 4096], P(None, 'hid'), may hold values from -0.078125 to 0.078125
- q_gain: float32 [4096], P('hid'), may hold values from 0.4 to 6
- k_gain: float32 [4096], P('hid'), may hold values from 0.4 to 6
- w_out: bfloat16 [4096, 5120], P('hid'), may hold values from -0.125 to 0.125
- w_up: bfloat16 [5120, 8192], P(None, 'hid'), may hold values from -0.078125 to 0.078125
- w_down: bfloat16 [8192, 5120], P('hid'), may hold values from -0.09375 to 0.09375
Outputs:
- block_out: bfloat16 [5120, 5120], P('seq', 'hid')
The draws below stay inside these ranges and needn't reach their ends.
Inputs may be any that keep to these rules, and one draw needn't show every extreme that they name: `clip_id`: clip numbers never fall along the tokens; every clip 0 to 7 holds 1 to 3200 tokens, and one holds exactly 3200.
All inputs are finite; a program needn't handle non-finite values.
Results may differ from the reference program's by a relative error of at most 0.018.
Values may be sent and summed in bfloat16 or wider, within the bound.
A program may use at most 128 MiB of HBM per device.

```python
import math
import jax
import jax.numpy as jnp
import numpy as np
from jax import lax

D = 5120
HEAD_DIM = 128
HEADS = 32
FF = 8192
TSTEPS = 32
TOK_DEV = 640
HD = 4096
TOKENS = 5120
CLIPS = 8
CLIP_MOST = 3200
N_SEQ = 8
N_HID = 16


def column_rise(col_count):
    return 3.0 ** (jnp.arange(col_count, dtype=jnp.float32) / col_count)


def draw_tokens(key, part):
    col_rise = column_rise(D)
    values = jax.random.truncated_normal(jax.random.fold_in(key, 13), -6.0, 6.0, (TOKENS, D), jnp.float32)
    return (values * col_rise[None, :]).astype(jnp.bfloat16)


def query_base(key):
    col_rise = column_rise(HD)
    fresh_rows = jax.random.truncated_normal(jax.random.fold_in(key, 21), -6.0, 6.0, (D, HD), jnp.float32)
    return fresh_rows * col_rise[None, :] / math.sqrt(D)


def draw_w_query(key, part):
    return query_base(key).astype(jnp.bfloat16)


def draw_w_key(key, part):
    col_rise = column_rise(HD)
    fresh_rows = jax.random.truncated_normal(jax.random.fold_in(key, 22), -6.0, 6.0, (D, HD), jnp.float32)
    fresh_rows = fresh_rows * col_rise[None, :] / math.sqrt(D)
    values = fresh_rows
    return values.astype(jnp.bfloat16)


def head_gains(key, salt_value, ceiling):
    levels = jax.random.uniform(jax.random.fold_in(key, salt_value), (HEADS,), jnp.float32)
    per_head = jnp.exp(math.log(0.5) + levels * (math.log(ceiling) - math.log(0.5)))
    ripple = jax.random.uniform(jax.random.fold_in(key, salt_value + 1), (HD,), jnp.float32, 0.9, 1.1)
    return jnp.repeat(per_head, HEAD_DIM) * ripple


def draw_q_gain(key, part):
    return head_gains(key, 31, 2.0)


def draw_k_gain(key, part):
    return head_gains(key, 41, 2.0)


def place_ends(result, own_key, smallest, top_value):
    dims = result.shape
    index_at = [jax.random.randint(jax.random.fold_in(own_key, axis), (), 0, dims[axis]) for axis in range(len(dims))]
    result = result.at[tuple(index_at)].set(smallest)
    longest = dims.index(max(dims))
    index_at[longest] = (index_at[longest] + 1) % dims[longest]
    return result.at[tuple(index_at)].set(top_value)


def raised(drawn, key, source, target, shards_of, factor):
    def block_of(axis_at):
        return (jnp.arange(drawn.shape[axis_at]) // (drawn.shape[axis_at] // shards_of)).reshape((-1,) + (1,) * (drawn.ndim - 1 - axis_at))

    near = jax.random.permutation(key, shards_of)[block_of(target)]
    other_side = (block_of(target) + shards_of // 2) % shards_of
    return jnp.where((block_of(source) == near) | (block_of(source) == other_side), factor * drawn, drawn)


def block_levels(stream_key, extent, shards, smallest, top_value):
    gain = 1.0
    for axis_at, shards_of in shards:
        draws = jax.random.uniform(jax.random.fold_in(jax.random.fold_in(stream_key, 6), axis_at), (shards_of,), jnp.float32, smallest / len(shards), top_value / len(shards))
        gain = gain * jnp.repeat(jnp.exp(draws), extent[axis_at] // shards_of).reshape((-1,) + (1,) * (len(extent) - 1 - axis_at))
    return gain


def split_up(number_of, total, bound, slope):
    weights = [(1 << 20) // math.isqrt(grade ** slope) + 1 for grade in range(2, number_of + 1)]
    rest, holding = total - bound - (number_of - 1), [1] * (number_of - 1)
    while rest > 0:
        candidates = [i for i in range(number_of - 1) if holding[i] < bound]
        pool, budget = sum([weights[i] for i in candidates]), rest
        for i in candidates:
            more = min(bound - holding[i], max(1, budget * weights[i] // pool), rest)
            holding[i] = holding[i] + more
            rest = rest - more
    return np.array([bound] + holding)


def ragged_sizes(rng, count, total, limit, slope):
    if count == 2:
        one = jax.random.randint(rng, (), max(1, total - limit), min(limit, total - 1) + 1)
        return jnp.stack([one, total - one])
    sizes = jnp.asarray(split_up(count, total, limit, slope), jnp.int32)
    pairs = (count - 1) // 2
    source_of, taker = sizes[1:1 + 2 * pairs:2], sizes[2:2 + 2 * pairs:2]
    slack = jnp.minimum(source_of - 1, limit - taker)
    passed = jax.random.randint(jax.random.fold_in(rng, 1), (pairs,), 0, 1 << 20) % (slack + 1)
    sizes = sizes.at[1:1 + 2 * pairs:2].set(source_of - passed).at[2:2 + 2 * pairs:2].set(taker + passed)
    return sizes[jax.random.permutation(jax.random.fold_in(rng, 2), count)]


def bell_draw(key, extent, deviation, limit, pieces=(), kind=jnp.bfloat16):
    factor_of = block_levels(key, extent, pieces, -0.22, 0.18) if pieces else 1.0
    values = jax.random.normal(key, extent, jnp.float32) * deviation * factor_of
    return jnp.minimum(jnp.maximum(values, -limit), limit).astype(kind)


def gaussian_with(own_key, shape, deviation, limit, split, heavy, held_as=jnp.bfloat16):
    array = deviation * jax.random.normal(own_key, shape, jnp.float32)
    if split:
        array = array * block_levels(own_key, shape, split, -0.22, 0.18)
    return jnp.clip(raised(array, jax.random.fold_in(own_key, 3), *heavy), -limit, limit).astype(held_as)


def setup_inputs(seed: int = 0) -> dict:
    arg_keys = jax.random.split(jax.random.key(seed), 13)
    return {
        "tokens": draw_tokens(jax.random.fold_in(arg_keys[12], 71), 0),
        "clip_id": jnp.searchsorted(jnp.cumsum(ragged_sizes(arg_keys[1], CLIPS, TOKENS, CLIP_MOST, 1)), jnp.arange(TOKENS), side="right").astype(jnp.int32),
        "clip_step": place_ends(jax.random.randint(arg_keys[2], (CLIPS,), 0, TSTEPS), jax.random.fold_in(arg_keys[2], 1), 0, TSTEPS - 1).astype(jnp.int32),
        "mod_table": bell_draw(arg_keys[3], (TSTEPS, 6, D), 0.5, 3.0, (), jnp.float32),
        "w_query": draw_w_query(jax.random.fold_in(arg_keys[12], 71), 0),
        "w_key": draw_w_key(jax.random.fold_in(arg_keys[12], 71), 0),
        "w_value": bell_draw(arg_keys[6], (D, HD), D ** -0.5, 0.078125, ((1, 16),)),
        "q_gain": draw_q_gain(jax.random.fold_in(arg_keys[12], 71), 0),
        "k_gain": draw_k_gain(jax.random.fold_in(arg_keys[12], 71), 0),
        "w_out": gaussian_with(arg_keys[9], (HD, D), HD ** -0.5, 0.125, ((0, 16),), (0, 1, 16, 2.0)),
        "w_up": bell_draw(arg_keys[10], (D, FF), D ** -0.5, 0.078125, ((1, 16),)),
        "w_down": gaussian_with(arg_keys[11], (FF, D), FF ** -0.5, 0.09375, ((0, 16),), (0, 1, 16, 2.0)),
    }


epsilon = 1e-06
masked_low = -1e+30

def layer_stats(values):
    row_mean = lax.optimization_barrier(jnp.mean(values, axis=1, keepdims=True))
    return (row_mean, lax.optimization_barrier(jnp.mean(values * values, axis=1, keepdims=True)) - row_mean * row_mean)

def modulate(values, mod_rows, shift_index):
    row_mean, spread_sq = layer_stats(values)
    scaled = (values - row_mean) * lax.rsqrt(spread_sq + epsilon)
    return (scaled * (1.0 + mod_rows[:, shift_index + 1, :]) + mod_rows[:, shift_index, :]).astype(jnp.bfloat16)

def grouped_sum(left, right):
    tok_rows = left.shape[0]
    left_groups = left.reshape(tok_rows, N_HID, -1).transpose(1, 0, 2).astype(jnp.float32)
    right_groups = right.reshape(N_HID, -1, right.shape[1]).astype(jnp.float32)
    partials = jnp.einsum('gtc,gcd->gtd', left_groups, right_groups)
    rounded = lax.optimization_barrier(partials.astype(jnp.bfloat16)).astype(jnp.float32)
    return lax.optimization_barrier(jnp.sum(rounded, axis=0))

def reference(tokens, clip_id, clip_step, mod_table, w_query, w_key, w_value, q_gain, k_gain, w_out, w_up, w_down):
    token_step = clip_step[clip_id]
    tok_blocks = tokens.reshape(N_SEQ, TOK_DEV, D)
    step_blocks = token_step.reshape(N_SEQ, TOK_DEV)

    def project(block_args):
        tok_block, step_block = block_args
        mod_rows = mod_table[step_block]
        normed = modulate(tok_block.astype(jnp.float32), mod_rows, 0)
        queries = jnp.dot(normed, w_query, preferred_element_type=jnp.float32)
        key_proj = jnp.dot(normed, w_key, preferred_element_type=jnp.float32)
        value_proj = jnp.dot(normed, w_value, preferred_element_type=jnp.float32)
        q_scale = lax.rsqrt(lax.optimization_barrier(jnp.mean(queries * queries, axis=1, keepdims=True)) + epsilon)
        k_scale = lax.rsqrt(lax.optimization_barrier(jnp.mean(key_proj * key_proj, axis=1, keepdims=True)) + epsilon)
        q_normed = (queries * q_scale * q_gain).astype(jnp.bfloat16)
        k_normed = (key_proj * k_scale * k_gain).astype(jnp.bfloat16)
        return (q_normed, k_normed, value_proj.astype(jnp.bfloat16))
    q_all, k_all, v_all = lax.map(project, (tok_blocks, step_blocks))
    q_heads = q_all.reshape(TOKENS, HEADS, HEAD_DIM).transpose(1, 0, 2)
    k_heads = k_all.reshape(TOKENS, HEADS, HEAD_DIM).transpose(1, 0, 2)
    v_heads = v_all.reshape(TOKENS, HEADS, HEAD_DIM).transpose(1, 0, 2)
    same_clip = clip_id[:, None] == clip_id[None, :]

    def head_attention(head_args):
        q_head, k_head, v_head = head_args
        scores = jnp.dot(q_head, k_head.T, preferred_element_type=jnp.float32) * HEAD_DIM ** (-0.5)
        masked = jnp.where(same_clip, scores, masked_low)
        row_best = lax.optimization_barrier(jnp.max(masked, axis=1, keepdims=True))
        weights = jnp.where(same_clip, jnp.exp(masked - row_best), 0.0)
        totals = lax.optimization_barrier(jnp.sum(weights, axis=1, keepdims=True))
        mixed = jnp.dot(weights.astype(jnp.bfloat16), v_head, preferred_element_type=jnp.float32)
        return (mixed / totals).astype(jnp.bfloat16)
    attended = lax.map(head_attention, (q_heads, k_heads, v_heads)).transpose(1, 0, 2).reshape(TOKENS, HD)
    attn_blocks = attended.reshape(N_SEQ, TOK_DEV, HD)

    def finish(block_args):
        tok_block, step_block, attn_block = block_args
        mod_rows = mod_table[step_block]
        attn_proj = grouped_sum(attn_block, w_out)
        residual = tok_block.astype(jnp.float32) + mod_rows[:, 2, :] * attn_proj
        residual = lax.optimization_barrier(residual.astype(jnp.bfloat16)).astype(jnp.float32)
        normed = modulate(residual, mod_rows, 3)
        hidden = jax.nn.gelu(jnp.dot(normed, w_up, preferred_element_type=jnp.float32), approximate=True).astype(jnp.bfloat16)
        ffn_proj = grouped_sum(hidden, w_down)
        return (residual + mod_rows[:, 5, :] * ffn_proj).astype(jnp.bfloat16)
    return lax.map(finish, (tok_blocks, step_blocks, attn_blocks)).reshape(TOKENS, D)
```

```python
import functools
import jax
import jax.numpy as jnp
from jax import lax
from jax.experimental import pallas as pl
from jax.experimental.pallas import tpu as pltpu

MESH = pl.DeviceIdType.MESH
HIGHEST = lax.Precision.HIGHEST
EPS = 1e-06
F32 = jnp.float32
BF16 = jnp.bfloat16
ANYSPEC = pl.BlockSpec(memory_space=pl.ANY)
VSPEC = pl.BlockSpec(memory_space=pltpu.VMEM)

OWN, XP, ZM, ZP, ZMX, ZPX, Z2, Z2X = range(8)
OFFSETS = ((0, 0), (0, 1), (3, 0), (1, 0), (3, 1), (1, 1), (2, 0), (2, 1))
BACK = (OWN, XP, ZP, ZM, ZPX, ZMX, Z2, Z2X)


def hid_place():
    h = lax.axis_index("hid")
    return h // 4, lax.rem(h // 2, 2), lax.rem(h, 2)


def chip_of(role):
    z, x, _ = hid_place()
    dz, dx = OFFSETS[role]
    return lax.rem(z + dz, 4) * 2 + lax.rem(x + dx, 2)


def hid_device(role, flip):
    core = hid_place()[2]
    core = 1 - core if flip else core
    return {"hid": chip_of(role) * 2 + core}


def rows_to_columns(rows, width):
    n = rows.shape[0]
    pick = (
        lax.broadcasted_iota(jnp.int32, (n, n * width), 1) // width
        == lax.broadcasted_iota(jnp.int32, (n, n * width), 0)
    ).astype(F32)
    return lax.dot_general(rows, pick, (((0,), (0,)), ((), ())), precision=HIGHEST, preferred_element_type=F32)


def lane_sums(values):
    ones = jnp.ones((8, values.shape[1]), F32)
    return lax.dot_general(ones, values, (((1,), (1,)), ((), ())), precision=HIGHEST, preferred_element_type=F32)[0:1]


def three_way(values):
    high = values.astype(BF16).astype(F32)
    rest = values - high
    middle = rest.astype(BF16).astype(F32)
    return jnp.concatenate([high, middle, rest - middle], axis=0).astype(BF16)


def gather_kernel(kind, widths, x_ref, hot_ref, mod_ref, *refs):
    nw = len(widths)
    w_refs, refs = refs[:nw], refs[nw:]
    if kind == "qkv":
        qg_ref, kg_ref, q_ref, k_ref, v_ref = refs[:5]
        refs = refs[5:]
    else:
        out_ref = refs[0]
        refs = refs[1:]
    (raw, nrm, pair, stat, wbuf, acc, wsem, psem, ssem, rsend, rrecv, dsend, drecv) = refs[:13]
    refs = refs[13:]
    half, full = raw.shape[1], raw.shape[2]
    part = full // 2
    quarter = half // 2
    core = hid_place()[2]
    total_w = sum(widths)

    w_copies = {}
    for role in (OWN, ZM, ZP, XP, Z2, ZMX, ZPX, Z2X):
        at = 0
        for i in range(nw):
            cp = pltpu.make_async_copy(
                w_refs[i].at[pl.ds(chip_of(role) * full, full)],
                wbuf.at[role, :, pl.ds(at, widths[i])],
                wsem.at[role, i],
            )
            cp.start()
            w_copies[role, i] = cp
            at += widths[i]

    barrier = pltpu.get_barrier_semaphore()
    n_peers = 8 if kind != "qkv" else 15
    pl.semaphore_signal(barrier, inc=1, device_id=hid_device(OWN, True), device_id_type=MESH)
    for role in range(1, 8):
        pl.semaphore_signal(barrier, inc=1, device_id=hid_device(role, False), device_id_type=MESH)
        if kind == "qkv":
            pl.semaphore_signal(barrier, inc=1, device_id=hid_device(role, True), device_id_type=MESH)
    pl.semaphore_wait(barrier, n_peers)

    swap = pltpu.make_async_remote_copy(
        x_ref.at[pl.ds((1 - core) * half, half)], pair, psem.at[0], psem.at[1],
        device_id=hid_device(OWN, True), device_id_type=MESH,
    )
    swap.start()
    sends = []

    def place(shift):
        rows = lax.broadcasted_iota(jnp.int32, (part, full), 0)
        cols = lax.broadcasted_iota(jnp.int32, (part, full), 1)
        return (cols == rows + shift).astype(F32).astype(BF16)

    mine = jnp.dot(x_ref[pl.ds(core * half, half)], place(core * part), preferred_element_type=F32)
    swap.wait_recv()
    block = mine + jnp.dot(pair[...], place((1 - core) * part), preferred_element_type=F32)
    raw[OWN] = block.astype(BF16)

    def send_raw(slot, lo, count, to_role, to_slot, sem):
        cp = pltpu.make_async_remote_copy(
            raw.at[slot, pl.ds(lo, count)], raw.at[to_slot, pl.ds(lo, count)],
            rsend.at[sem], rrecv.at[sem],
            device_id=hid_device(to_role, False), device_id_type=MESH,
        )
        cp.start()
        sends.append(cp)
        return cp

    to_zp = send_raw(OWN, 0, half, ZP, ZM, ZM)
    to_zm = send_raw(OWN, 0, half, ZM, ZP, ZP)
    to_x = send_raw(OWN, 0, half, XP, XP, XP)

    stat[OWN, 0:1] = lane_sums(block)
    stat[OWN, 1:2] = lane_sums(block * block)
    stat_copies = []
    for role in range(1, 8):
        cp = pltpu.make_async_remote_copy(
            stat.at[OWN], stat.at[BACK[role]], ssem.at[0, role], ssem.at[1, BACK[role]],
            device_id=hid_device(role, False), device_id_type=MESH,
        )
        cp.start()
        stat_copies.append(cp)
    for cp in stat_copies:
        cp.wait()
    totals = stat[0]
    for role in range(1, 8):
        totals = totals + stat[role]
    width_all = full * 8
    moments = rows_to_columns(totals * (1.0 / width_all), 128)
    row_mean = moments[:, 0:1]
    inv = lax.rsqrt(moments[:, 128:129] - row_mean * row_mean + EPS)
    hot = hot_ref[pl.ds(core * half, half)]
    d_copies = {}

    def normalize(role):
        col = pl.multiple_of(chip_of(role) * full, 128)
        scale = jnp.dot(hot, three_way(mod_ref[0, :, pl.ds(col, full)]), preferred_element_type=F32)
        shift = jnp.dot(hot, three_way(mod_ref[1, :, pl.ds(col, full)]), preferred_element_type=F32)
        values = (raw[role].astype(F32) - row_mean) * inv
        nrm[core, role] = (values * (1.0 + scale) + shift).astype(BF16)
        cp = pltpu.make_async_remote_copy(
            nrm.at[core, role], nrm.at[core, role], dsend.at[role], drecv.at[role],
            device_id=hid_device(OWN, True), device_id_type=MESH,
        )
        cp.start()
        d_copies[role] = cp

    first = [True, True]

    def multiply(role, which):
        side = core if which == 0 else 1 - core
        if which == 0:
            for i in range(nw):
                w_copies[role, i].wait()
        else:
            d_copies[role].wait_recv()
        term = jnp.dot(nrm[side, role], wbuf[role], preferred_element_type=F32)
        if first[which]:
            acc[side] = term
        else:
            acc[side] += term
        first[which] = False

    normalize(OWN)
    multiply(OWN, 0)
    to_zp.wait_recv()
    send_raw(ZM, 0, quarter, ZP, Z2, Z2)
    to_zm.wait_recv()
    send_raw(ZP, quarter, quarter, ZM, Z2, 8)
    to_x.wait_recv()
    send_raw(XP, 0, half, ZP, ZMX, ZMX)
    send_raw(XP, 0, half, ZM, ZPX, ZPX)
    multiply(OWN, 1)
    normalize(ZM)
    multiply(ZM, 0)
    normalize(ZP)
    multiply(ZP, 0)
    multiply(ZM, 1)
    normalize(XP)
    multiply(XP, 0)
    multiply(ZP, 1)
    sends[3].wait_recv()
    sends[4].wait_recv()
    send_raw(Z2, 0, half, XP, Z2X, Z2X)
    multiply(XP, 1)
    normalize(Z2)
    multiply(Z2, 0)
    multiply(Z2, 1)
    sends[5].wait_recv()
    normalize(ZMX)
    multiply(ZMX, 0)
    sends[6].wait_recv()
    normalize(ZPX)
    multiply(ZPX, 0)
    multiply(ZMX, 1)
    sends[7].wait_recv()
    normalize(Z2X)
    multiply(Z2X, 0)
    multiply(ZPX, 1)
    multiply(Z2X, 1)

    swap.wait_send()
    for cp in sends:
        cp.wait_send()
    for role in range(8):
        d_copies[role].wait_send()

    if kind != "qkv":
        for side in range(2):
            out_ref[pl.ds(side * half, half)] = jax.nn.gelu(acc[side], approximate=True).astype(BF16)
        return

    qstat, qsend, qrecv = refs
    wq = widths[0]
    for side in range(2):
        q = acc[side, :, 0:wq]
        k = acc[side, :, wq:2 * wq]
        qstat[0, 2 * side:2 * side + 1] = lane_sums(q * q)
        qstat[0, 2 * side + 1:2 * side + 2] = lane_sums(k * k)
        v_ref[pl.ds(side * half, half)] = acc[side, :, 2 * wq:3 * wq].astype(BF16)
    copies = []
    for flip in (False, True):
        for role in range(8):
            if role == OWN and not flip:
                continue
            cp = pltpu.make_async_remote_copy(
                qstat.at[0], qstat.at[BACK[role] + 8 * flip], qsend.at[role + 8 * flip], qrecv.at[BACK[role] + 8 * flip],
                device_id=hid_device(role, flip), device_id_type=MESH,
            )
            cp.start()
            copies.append(cp)
    for cp in copies:
        cp.wait()
    sums = qstat[0]
    for i in range(1, 16):
        sums = sums + qstat[i]
    scales = lax.rsqrt(rows_to_columns(sums * (1.0 / (16 * wq)), 128) + EPS)
    for side in range(2):
        at = side * 256
        q_ref[pl.ds(side * half, half)] = (acc[side, :, 0:wq] * scales[:, at:at + 1] * qg_ref[...]).astype(BF16)
        k_ref[pl.ds(side * half, half)] = (acc[side, :, wq:2 * wq] * scales[:, at + 128:at + 129] * kg_ref[...]).astype(BF16)


def gather_project(kind, x, hot, mod, weights, gains, cid):
    rows, part = x.shape
    half, full = rows // 2, 2 * part
    widths = tuple(w.shape[1] for w in weights)
    total = sum(widths)
    if kind == "qkv":
        outs = [jax.ShapeDtypeStruct((rows, w), BF16) for w in widths]
        extra = [pltpu.VMEM((16, 4, half), F32), pltpu.SemaphoreType.DMA((16,)), pltpu.SemaphoreType.DMA((16,))]
    else:
        outs = [jax.ShapeDtypeStruct((rows, total), BF16)]
        extra = []
    res = pl.pallas_call(
        functools.partial(gather_kernel, kind, widths),
        out_shape=outs,
        in_specs=[VSPEC, VSPEC, VSPEC] + [ANYSPEC] * len(weights) + [VSPEC] * len(gains),
        out_specs=[VSPEC] * len(outs),
        scratch_shapes=[
            pltpu.VMEM((8, half, full), BF16),
            pltpu.VMEM((2, 8, half, full), BF16),
            pltpu.VMEM((half, part), BF16),
            pltpu.VMEM((8, 2, half), F32),
            pltpu.VMEM((8, full, total), BF16),
            pltpu.VMEM((2, half, total), F32),
            pltpu.SemaphoreType.DMA((8, len(weights))),
            pltpu.SemaphoreType.DMA((2,)),
            pltpu.SemaphoreType.DMA((2, 8)),
            pltpu.SemaphoreType.DMA((9,)),
            pltpu.SemaphoreType.DMA((9,)),
            pltpu.SemaphoreType.DMA((8,)),
            pltpu.SemaphoreType.DMA((8,)),
        ] + extra,
        compiler_params=pltpu.CompilerParams(collective_id=cid, has_side_effects=True, vmem_limit_bytes=56 << 20),
        name="gather_" + kind,
    )(x, hot, mod, *weights, *gains)
    return res
from jax.sharding import PartitionSpec as P
HEAD_DIM = 128


epsilon = 1e-06
highest = lax.Precision.HIGHEST
masked_low = -1e30


def table_rows(step_hot, mod_table, component, col_start, col_count):
    table = lax.dynamic_slice_in_dim(mod_table[:, component, :], col_start, col_count, 1)
    return jnp.dot(step_hot, table, precision=highest, preferred_element_type=jnp.float32)


def modulated(values, row_mean, spread_sq, scale_rows, shift_rows):
    scaled = (values - row_mean) * lax.rsqrt(spread_sq + epsilon)
    return (scaled * (1.0 + scale_rows) + shift_rows).astype(jnp.bfloat16)


def shared_moments(values, full_width):
    summed, squares = lax.psum((jnp.sum(values, axis=1), jnp.sum(values * values, axis=1)), "hid")
    row_mean = (summed / full_width)[:, None]
    return (row_mean, (squares / full_width)[:, None] - row_mean * row_mean)


def stored(values):
    return lax.optimization_barrier(values.astype(jnp.bfloat16)).astype(jnp.float32)


def shards(
    tokens,
    clip_id,
    clip_step,
    mod_table,
    w_query,
    w_key,
    w_value,
    q_gain,
    k_gain,
    w_out,
    w_up,
    w_down,
):
    tok_rows, feat_part = tokens.shape
    full_width = mod_table.shape[2]
    col_start = lax.axis_index("hid") * feat_part
    head_cols = w_query.shape[1]
    heads_here = head_cols // HEAD_DIM
    all_cols = head_cols * lax.axis_size("hid")
    clip_hot = (
        clip_id[:, None] == jnp.arange(clip_step.shape[0], dtype=jnp.int32)[None, :]
    ).astype(jnp.float32)
    token_step = jnp.dot(
        clip_hot,
        clip_step.astype(jnp.float32),
        precision=highest,
        preferred_element_type=jnp.float32,
    )
    step_hot = (
        token_step[:, None] == jnp.arange(mod_table.shape[0], dtype=jnp.float32)[None, :]
    ).astype(jnp.float32)
    own_rows = tokens.astype(jnp.float32)
    gate_ffn = table_rows(step_hot, mod_table, 5, col_start, feat_part)
    mods = mod_table[clip_step].transpose(1, 0, 2)
    hot24 = (clip_id[:, None] == jnp.arange(24, dtype=jnp.int32)[None, :] % 8).astype(jnp.bfloat16)
    q_normed, k_normed, value_rows = gather_project(
        "qkv", tokens, hot24, jnp.stack([mods[1], mods[0]]), (w_query, w_key, w_value),
        (q_gain[None, :], k_gain[None, :]), 1,
    )
    clip_marks = clip_id.astype(jnp.bfloat16)
    q_heads = q_normed.reshape(tok_rows, heads_here, HEAD_DIM)
    score_scale = HEAD_DIM ** (-0.5)

    def tile_update(running, tile):
        key_tile, value_tile, mark_tile = tile
        old_best, old_sum, old_acc = running
        scores = (
            jnp.einsum("qhd,khd->hqk", q_heads, key_tile, preferred_element_type=jnp.float32)
            * score_scale
        )
        same_clip = (clip_marks[:, None] == mark_tile[None, :])[None]
        masked = jnp.where(same_clip, scores, masked_low)
        row_best = jnp.maximum(old_best, jnp.max(masked, axis=2))
        weights = jnp.where(same_clip, jnp.exp(masked - row_best[:, :, None]), 0.0)
        rescale = jnp.exp(old_best - row_best)
        new_sum = old_sum * rescale + jnp.sum(weights, axis=2)
        mixed = jnp.einsum(
            "hqk,khd->hqd",
            weights.astype(jnp.bfloat16),
            value_tile,
            preferred_element_type=jnp.float32,
        )
        return (row_best, new_sum, old_acc * rescale[:, :, None] + mixed)

    start_state = (
        jnp.full((heads_here, tok_rows), masked_low, jnp.float32),
        jnp.zeros((heads_here, tok_rows), jnp.float32),
        jnp.zeros((heads_here, tok_rows, HEAD_DIM), jnp.float32),
    )
    key_piece = lax.all_gather(k_normed, "seq", axis=0, tiled=True)
    value_piece = lax.all_gather(value_rows, "seq", axis=0, tiled=True)
    mark_piece = lax.all_gather(clip_marks, "seq", axis=0, tiled=True)
    tile_count = key_piece.shape[0] // tok_rows
    tiles = (
        key_piece.reshape(tile_count, tok_rows, heads_here, HEAD_DIM),
        value_piece.reshape(tile_count, tok_rows, heads_here, HEAD_DIM),
        mark_piece.reshape(tile_count, tok_rows),
    )

    def tile_step(inner, tile):
        return (tile_update(inner, tile), None)

    finished, unused = lax.scan(tile_step, start_state, tiles)
    best_all, sum_all, acc_all = finished
    attended = (
        (acc_all / sum_all[:, :, None])
        .astype(jnp.bfloat16)
        .transpose(1, 0, 2)
        .reshape(tok_rows, head_cols)
    )
    out_terms = jnp.dot(attended, w_out, preferred_element_type=jnp.float32)
    attn_own = lax.psum_scatter(
        out_terms.astype(jnp.bfloat16), "hid", scatter_dimension=1, tiled=True
    ).astype(jnp.float32)
    gate_attn = table_rows(step_hot, mod_table, 2, col_start, feat_part)
    residual_own = stored(own_rows + gate_attn * attn_own)
    row_mean, spread_sq = shared_moments(residual_own, full_width)
    normed_ffn = modulated(
        residual_own,
        row_mean,
        spread_sq,
        table_rows(step_hot, mod_table, 4, col_start, feat_part),
        table_rows(step_hot, mod_table, 3, col_start, feat_part),
    )
    up_proj = jnp.dot(
        lax.all_gather(normed_ffn, "hid", axis=1, tiled=True),
        w_up,
        preferred_element_type=jnp.float32,
    )
    hidden = jax.nn.gelu(up_proj, approximate=True).astype(jnp.bfloat16)
    ffn_own = lax.psum_scatter(
        jnp.dot(hidden, w_down, preferred_element_type=jnp.float32).astype(jnp.bfloat16),
        "hid",
        scatter_dimension=1,
        tiled=True,
    ).astype(jnp.float32)
    return (residual_own + gate_ffn * ffn_own).astype(jnp.bfloat16)


def solution(mesh):
    placed = (
        P("seq", "hid"),
        P("seq"),
        P(),
        P(),
        P(None, "hid"),
        P(None, "hid"),
        P(None, "hid"),
        P("hid"),
        P("hid"),
        P("hid", None),
        P(None, "hid"),
        P("hid", None),
    )
    return jax.shard_map(
        shards, mesh=mesh, in_specs=placed, out_specs=P("seq", "hid"), check_vma=False
    )
```

```python
import functools
import jax
import jax.numpy as jnp
from jax import lax
from jax.experimental import pallas as pl
from jax.experimental.pallas import tpu as pltpu
from jax.sharding import PartitionSpec as P

MESH = pl.DeviceIdType.MESH
HIGHEST = lax.Precision.HIGHEST
EPS = 1e-06
SCORE_SCALE = 128 ** (-0.5) * 1.4426950408889634
F32 = jnp.float32
BF16 = jnp.bfloat16
ANYSPEC = pl.BlockSpec(memory_space=pl.ANY)
VSPEC = pl.BlockSpec(memory_space=pltpu.VMEM)

OWN, XP, ZM, ZP, ZMX, ZPX, Z2, Z2X = range(8)
OFFSETS = ((0, 0), (0, 1), (3, 0), (1, 0), (3, 1), (1, 1), (2, 0), (2, 1))
BACK = (OWN, XP, ZP, ZM, ZPX, ZMX, Z2, Z2X)


def hid_place():
    h = lax.axis_index("hid")
    return h // 4, lax.rem(h // 2, 2), lax.rem(h, 2)


def chip_of(role):
    z, x, _ = hid_place()
    dz, dx = OFFSETS[role]
    return lax.rem(z + dz, 4) * 2 + lax.rem(x + dx, 2)


def hid_device(role, flip):
    core = hid_place()[2]
    core = 1 - core if flip else core
    return {"hid": chip_of(role) * 2 + core}


def rows_to_columns(rows, width):
    n = rows.shape[0]
    pick = (
        lax.broadcasted_iota(jnp.int32, (n, n * width), 1) // width
        == lax.broadcasted_iota(jnp.int32, (n, n * width), 0)
    ).astype(F32)
    return lax.dot_general(rows, pick, (((0,), (0,)), ((), ())), precision=HIGHEST, preferred_element_type=F32)


def lane_sums(values):
    ones = jnp.ones((8, values.shape[1]), F32)
    return lax.dot_general(ones, values, (((1,), (1,)), ((), ())), precision=HIGHEST, preferred_element_type=F32)[0:1]


def three_way(values):
    high = values.astype(BF16).astype(F32)
    rest = values - high
    middle = rest.astype(BF16).astype(F32)
    return jnp.concatenate([high, middle, rest - middle], axis=0).astype(BF16)


def gather_kernel(kind, widths, x_ref, hot_ref, mod_ref, *refs):
    nw = len(widths)
    w_refs, refs = refs[:nw], refs[nw:]
    if kind == "qkv":
        qg_ref, kg_ref, q_ref, k_ref, v_ref = refs[:5]
        refs = refs[5:]
    else:
        out_ref = refs[0]
        refs = refs[1:]
    (raw, nrm, pair, stat, wbuf, acc, wsem, psem, ssem, rsend, rrecv, dsend, drecv) = refs[:13]
    refs = refs[13:]
    half, full = raw.shape[1], raw.shape[2]
    part = full // 2
    quarter = half // 2
    core = hid_place()[2]
    total_w = sum(widths)

    w_copies = {}
    for role in (OWN, ZM, ZP, XP, Z2, ZMX, ZPX, Z2X):
        at = 0
        for i in range(nw):
            cp = pltpu.make_async_copy(
                w_refs[i].at[pl.ds(chip_of(role) * full, full)],
                wbuf.at[role, :, pl.ds(at, widths[i])],
                wsem.at[role, i],
            )
            cp.start()
            w_copies[role, i] = cp
            at += widths[i]

    barrier = pltpu.get_barrier_semaphore()
    n_peers = 8 if kind != "qkv" else 15
    pl.semaphore_signal(barrier, inc=1, device_id=hid_device(OWN, True), device_id_type=MESH)
    for role in range(1, 8):
        pl.semaphore_signal(barrier, inc=1, device_id=hid_device(role, False), device_id_type=MESH)
        if kind == "qkv":
            pl.semaphore_signal(barrier, inc=1, device_id=hid_device(role, True), device_id_type=MESH)
    pl.semaphore_wait(barrier, n_peers)

    swap = pltpu.make_async_remote_copy(
        x_ref.at[pl.ds((1 - core) * half, half)], pair, psem.at[0], psem.at[1],
        device_id=hid_device(OWN, True), device_id_type=MESH,
    )
    swap.start()
    sends = []

    def place(shift):
        rows = lax.broadcasted_iota(jnp.int32, (part, full), 0)
        cols = lax.broadcasted_iota(jnp.int32, (part, full), 1)
        return (cols == rows + shift).astype(F32).astype(BF16)

    mine = jnp.dot(x_ref[pl.ds(core * half, half)], place(core * part), preferred_element_type=F32)
    swap.wait_recv()
    block = mine + jnp.dot(pair[...], place((1 - core) * part), preferred_element_type=F32)
    raw[OWN] = block.astype(BF16)

    def send_raw(slot, lo, count, to_role, to_slot, sem):
        cp = pltpu.make_async_remote_copy(
            raw.at[slot, pl.ds(lo, count)], raw.at[to_slot, pl.ds(lo, count)],
            rsend.at[sem], rrecv.at[sem],
            device_id=hid_device(to_role, False), device_id_type=MESH,
        )
        cp.start()
        sends.append(cp)
        return cp

    to_zp = send_raw(OWN, 0, half, ZP, ZM, ZM)
    to_zm = send_raw(OWN, 0, half, ZM, ZP, ZP)
    to_x = send_raw(OWN, 0, half, XP, XP, XP)

    stat[OWN, 0:1] = lane_sums(block)
    stat[OWN, 1:2] = lane_sums(block * block)
    stat_copies = []
    for role in range(1, 8):
        cp = pltpu.make_async_remote_copy(
            stat.at[OWN], stat.at[BACK[role]], ssem.at[0, role], ssem.at[1, BACK[role]],
            device_id=hid_device(role, False), device_id_type=MESH,
        )
        cp.start()
        stat_copies.append(cp)
    for cp in stat_copies:
        cp.wait()
    totals = stat[0]
    for role in range(1, 8):
        totals = totals + stat[role]
    width_all = full * 8
    moments = rows_to_columns(totals * (1.0 / width_all), 128)
    row_mean = moments[:, 0:1]
    inv = lax.rsqrt(moments[:, 128:129] - row_mean * row_mean + EPS)
    hot = hot_ref[pl.ds(core * half, half)]
    d_copies = {}

    def normalize(role):
        col = pl.multiple_of(chip_of(role) * full, 128)
        scale = jnp.dot(hot, three_way(mod_ref[0, :, pl.ds(col, full)]), preferred_element_type=F32)
        shift = jnp.dot(hot, three_way(mod_ref[1, :, pl.ds(col, full)]), preferred_element_type=F32)
        values = (raw[role].astype(F32) - row_mean) * inv
        nrm[core, role] = (values * (1.0 + scale) + shift).astype(BF16)
        cp = pltpu.make_async_remote_copy(
            nrm.at[core, role], nrm.at[core, role], dsend.at[role], drecv.at[role],
            device_id=hid_device(OWN, True), device_id_type=MESH,
        )
        cp.start()
        d_copies[role] = cp

    first = [True, True]

    def multiply(role, which):
        side = core if which == 0 else 1 - core
        if which == 0:
            for i in range(nw):
                w_copies[role, i].wait()
        else:
            d_copies[role].wait_recv()
        term = jnp.dot(nrm[side, role], wbuf[role], preferred_element_type=F32)
        if first[which]:
            acc[side] = term
        else:
            acc[side] += term
        first[which] = False

    normalize(OWN)
    multiply(OWN, 0)
    to_zp.wait_recv()
    send_raw(ZM, 0, quarter, ZP, Z2, Z2)
    to_zm.wait_recv()
    send_raw(ZP, quarter, quarter, ZM, Z2, 8)
    to_x.wait_recv()
    send_raw(XP, 0, half, ZP, ZMX, ZMX)
    send_raw(XP, 0, half, ZM, ZPX, ZPX)
    multiply(OWN, 1)
    normalize(ZM)
    multiply(ZM, 0)
    normalize(ZP)
    multiply(ZP, 0)
    multiply(ZM, 1)
    normalize(XP)
    multiply(XP, 0)
    multiply(ZP, 1)
    sends[3].wait_recv()
    sends[4].wait_recv()
    send_raw(Z2, 0, half, XP, Z2X, Z2X)
    multiply(XP, 1)
    normalize(Z2)
    multiply(Z2, 0)
    multiply(Z2, 1)
    sends[5].wait_recv()
    normalize(ZMX)
    multiply(ZMX, 0)
    sends[6].wait_recv()
    normalize(ZPX)
    multiply(ZPX, 0)
    multiply(ZMX, 1)
    sends[7].wait_recv()
    normalize(Z2X)
    multiply(Z2X, 0)
    multiply(ZPX, 1)
    multiply(Z2X, 1)

    swap.wait_send()
    for cp in sends:
        cp.wait_send()
    for role in range(8):
        d_copies[role].wait_send()

    if kind != "qkv":
        for side in range(2):
            out_ref[pl.ds(side * half, half)] = jax.nn.gelu(acc[side], approximate=True).astype(BF16)
        return

    qstat, qsend, qrecv = refs
    wq = widths[0]
    for side in range(2):
        q = acc[side, :, 0:wq]
        k = acc[side, :, wq:2 * wq]
        qstat[0, 2 * side:2 * side + 1] = lane_sums(q * q)
        qstat[0, 2 * side + 1:2 * side + 2] = lane_sums(k * k)
        v_ref[pl.ds(side * half, half)] = acc[side, :, 2 * wq:3 * wq].astype(BF16)
    copies = []
    for flip in (False, True):
        for role in range(8):
            if role == OWN and not flip:
                continue
            cp = pltpu.make_async_remote_copy(
                qstat.at[0], qstat.at[BACK[role] + 8 * flip], qsend.at[role + 8 * flip], qrecv.at[BACK[role] + 8 * flip],
                device_id=hid_device(role, flip), device_id_type=MESH,
            )
            cp.start()
            copies.append(cp)
    for cp in copies:
        cp.wait()
    sums = qstat[0]
    for i in range(1, 16):
        sums = sums + qstat[i]
    scales = lax.rsqrt(rows_to_columns(sums * (1.0 / (16 * wq)), 128) + EPS)
    for side in range(2):
        at = side * 256
        q_ref[pl.ds(side * half, half)] = (
            acc[side, :, 0:wq] * (scales[:, at:at + 1] * SCORE_SCALE) * qg_ref[...]
        ).astype(BF16)
        k_ref[pl.ds(side * half, half)] = (acc[side, :, wq:2 * wq] * scales[:, at + 128:at + 129] * kg_ref[...]).astype(BF16)


def gather_project(kind, x, hot, mod, weights, gains, cid):
    rows, part = x.shape
    half, full = rows // 2, 2 * part
    widths = tuple(w.shape[1] for w in weights)
    total = sum(widths)
    if kind == "qkv":
        outs = [jax.ShapeDtypeStruct((rows, w), BF16) for w in widths]
        extra = [pltpu.VMEM((16, 4, half), F32), pltpu.SemaphoreType.DMA((16,)), pltpu.SemaphoreType.DMA((16,))]
    else:
        outs = [jax.ShapeDtypeStruct((rows, total), BF16)]
        extra = []
    res = pl.pallas_call(
        functools.partial(gather_kernel, kind, widths),
        out_shape=outs,
        in_specs=[VSPEC, VSPEC, VSPEC] + [ANYSPEC] * len(weights) + [VSPEC] * len(gains),
        out_specs=[VSPEC] * len(outs),
        scratch_shapes=[
            pltpu.VMEM((8, half, full), BF16),
            pltpu.VMEM((2, 8, half, full), BF16),
            pltpu.VMEM((half, part), BF16),
            pltpu.VMEM((8, 2, half), F32),
            pltpu.VMEM((8, full, total), BF16),
            pltpu.VMEM((2, half, total), F32),
            pltpu.SemaphoreType.DMA((8, len(weights))),
            pltpu.SemaphoreType.DMA((2,)),
            pltpu.SemaphoreType.DMA((2, 8)),
            pltpu.SemaphoreType.DMA((9,)),
            pltpu.SemaphoreType.DMA((9,)),
            pltpu.SemaphoreType.DMA((8,)),
            pltpu.SemaphoreType.DMA((8,)),
        ] + extra,
        compiler_params=pltpu.CompilerParams(collective_id=cid, has_side_effects=True, vmem_limit_bytes=56 << 20),
        name="gather_" + kind,
    )(x, hot, mod, *weights, *gains)
    return res


Y_STEPS = (0, 3, 1, 2)
Y_BACK = (0, 2, 1, 3)
HEAD_DIM = 128
FAR = -1e30


def seq_device(y_role, flip):
    s = lax.axis_index("seq")
    y, x = s // 2, lax.rem(s, 2)
    x = 1 - x if flip else x
    return {"seq": lax.rem(y + Y_STEPS[y_role], 4) * 2 + x}


def attend_kernel(q_ref, k_ref, v_ref, clip_ref, out_ref, qb, kb, vb, crow, best, acc, obuf,
                  xsend, xrecv, ysend, yrecv, csend, crecv, osem):
    rows = q_ref.shape[0]
    tile = rows // 2
    xh = lax.rem(lax.axis_index("seq"), 2)
    mine = pl.ds(pl.multiple_of(xh * HEAD_DIM, HEAD_DIM), HEAD_DIM)
    other = pl.ds(pl.multiple_of((1 - xh) * HEAD_DIM, HEAD_DIM), HEAD_DIM)
    low = pl.ds(0, HEAD_DIM)
    high = pl.ds(HEAD_DIM, HEAD_DIM)
    peers = [(y, f) for y in range(4) for f in (0, 1) if (y, f) != (0, 0)]

    barrier = pltpu.get_barrier_semaphore()
    for y, f in peers:
        pl.semaphore_signal(barrier, inc=1, device_id=seq_device(y, f), device_id_type=MESH)

    vb[0, :, 0:HEAD_DIM] = v_ref[:, mine]
    kb[0, :, 0:HEAD_DIM] = k_ref[:, mine]
    qb[pl.ds(0, rows), 0:HEAD_DIM] = q_ref[:, mine]
    crow[0] = clip_ref[...]
    pl.semaphore_wait(barrier, len(peers))

    started = []

    def send(src, dst, send_sem, recv_sem, y, f):
        cp = pltpu.make_async_remote_copy(src, dst, send_sem, recv_sem, device_id=seq_device(y, f), device_id_type=MESH)
        cp.start()
        started.append(cp)
        return cp

    clips = [
        send(crow.at[0], crow.at[Y_BACK[y] * 2 + f], csend.at[y * 2 + f], crecv.at[Y_BACK[y] * 2 + f], y, f)
        for y, f in peers
    ]
    x_k = send(k_ref.at[:, other], kb.at[1, :, low], xsend.at[0], xrecv.at[0], 0, 1)
    x_v = send(v_ref.at[:, other], vb.at[1, :, low], xsend.at[1], xrecv.at[1], 0, 1)

    def send_y(buf, which, slot, y_role, to_slot):
        return send(
            buf.at[slot, :, low], buf.at[to_slot, :, low],
            ysend.at[which, to_slot], yrecv.at[which, to_slot], y_role, 0,
        )

    ys = {}
    for f in (0,):
        ys["k", 2 + f] = send_y(kb, 0, f, 2, 2 + f)
        ys["k", 4 + f] = send_y(kb, 0, f, 1, 4 + f)
        ys["v", 2 + f] = send_y(vb, 1, f, 2, 2 + f)
        ys["v", 4 + f] = send_y(vb, 1, f, 1, 4 + f)
    x_q = send(q_ref.at[:, other], qb.at[pl.ds(rows, rows), low], xsend.at[2], xrecv.at[2], 0, 1)

    lane = lax.broadcasted_iota(jnp.int32, (rows, HEAD_DIM), 1).astype(F32)

    def clip_columns(slot):
        return rows_to_columns(crow[slot], HEAD_DIM)

    def mark_keys(slot):
        kb[slot, :, HEAD_DIM:2 * HEAD_DIM] = jnp.where(clip_columns(slot) == lane, 0.0, FAR).astype(BF16)
        vb[slot, :, HEAD_DIM:2 * HEAD_DIM] = jnp.ones((rows, HEAD_DIM), BF16)

    def mark_queries(side):
        qb[pl.ds(side * rows, rows), HEAD_DIM:2 * HEAD_DIM] = (clip_columns(side) == lane).astype(F32).astype(BF16)

    def attend(slot, start, stop, first=False):
        def step(t, carry):
            at = pl.ds(pl.multiple_of(t * tile, tile), tile)
            scores = lax.dot_general(qb[at], kb[slot], (((1,), (1,)), ((), ())), preferred_element_type=F32)
            top = jnp.max(scores, axis=1, keepdims=True)
            if first:
                fresh = top
            else:
                old = best[at][:, 0:1]
                fresh = jnp.maximum(old, top)
            weights = jnp.exp2(scores - fresh).astype(BF16)
            mixed = jnp.dot(weights, vb[slot], preferred_element_type=F32)
            if first:
                acc[at] = mixed
            else:
                acc[at] = acc[at] * jnp.exp2(old - fresh) + mixed
            best[at] = jnp.broadcast_to(fresh, (tile, HEAD_DIM))
            return carry

        lax.fori_loop(start, stop, step, 0)

    mark_keys(0)
    mark_queries(0)
    attend(0, 0, 2, True)
    x_k.wait_recv()
    ys["k", 3] = send_y(kb, 0, 1, 2, 3)
    ys["k", 5] = send_y(kb, 0, 1, 1, 5)
    x_v.wait_recv()
    ys["v", 3] = send_y(vb, 1, 1, 2, 3)
    ys["v", 5] = send_y(vb, 1, 1, 1, 5)
    ys["k", 2].wait_recv()
    ys["k", 6] = send_y(kb, 0, 2, 2, 6)
    ys["k", 4].wait_recv()
    ys["v", 4].wait_recv()
    ys["v", 6] = send_y(vb, 1, 4, 1, 6)
    ys["v", 2].wait_recv()
    for cp in clips:
        cp.wait_recv()
    mark_keys(1)
    attend(1, 0, 2)
    mark_keys(2)
    attend(2, 0, 2)
    mark_keys(4)
    attend(4, 0, 2)
    x_q.wait_recv()
    mark_queries(1)
    attend(1, 2, 4, True)
    ys["k", 3].wait_recv()
    ys["k", 7] = send_y(kb, 0, 3, 2, 7)
    ys["v", 5].wait_recv()
    ys["v", 7] = send_y(vb, 1, 5, 1, 7)
    attend(0, 2, 4)
    attend(2, 2, 4)
    attend(4, 2, 4)
    ys["v", 3].wait_recv()
    ys["k", 5].wait_recv()
    mark_keys(3)
    attend(3, 0, 4)
    mark_keys(5)
    attend(5, 0, 4)
    ys["k", 6].wait_recv()
    ys["v", 6].wait_recv()
    mark_keys(6)
    attend(6, 0, 4)
    ys["k", 7].wait_recv()
    ys["v", 7].wait_recv()
    mark_keys(7)
    attend(7, 2, 4)
    obuf[...] = (acc[pl.ds(rows, rows), 0:HEAD_DIM] / acc[pl.ds(rows, rows), HEAD_DIM:2 * HEAD_DIM]).astype(BF16)
    back = send(obuf, out_ref.at[:, mine], osem.at[0], osem.at[1], 0, 1)
    attend(7, 0, 2)
    out_ref[:, mine] = (acc[pl.ds(0, rows), 0:HEAD_DIM] / acc[pl.ds(0, rows), HEAD_DIM:2 * HEAD_DIM]).astype(BF16)
    back.wait_recv()
    for cp in started:
        cp.wait_send()


def attend(q, k, v, clip_row, cid):
    rows, cols = q.shape
    return pl.pallas_call(
        attend_kernel,
        out_shape=jax.ShapeDtypeStruct((rows, cols), BF16),
        in_specs=[VSPEC] * 4,
        out_specs=VSPEC,
        scratch_shapes=[
            pltpu.VMEM((2 * rows, 2 * HEAD_DIM), BF16),
            pltpu.VMEM((8, rows, 2 * HEAD_DIM), BF16),
            pltpu.VMEM((8, rows, 2 * HEAD_DIM), BF16),
            pltpu.VMEM((8, 1, rows), F32),
            pltpu.VMEM((2 * rows, HEAD_DIM), F32),
            pltpu.VMEM((2 * rows, 2 * HEAD_DIM), F32),
            pltpu.VMEM((rows, HEAD_DIM), BF16),
            pltpu.SemaphoreType.DMA((3,)),
            pltpu.SemaphoreType.DMA((3,)),
            pltpu.SemaphoreType.DMA((2, 8)),
            pltpu.SemaphoreType.DMA((2, 8)),
            pltpu.SemaphoreType.DMA((8,)),
            pltpu.SemaphoreType.DMA((8,)),
            pltpu.SemaphoreType.DMA((2,)),
        ],
        compiler_params=pltpu.CompilerParams(collective_id=cid, has_side_effects=True, vmem_limit_bytes=48 << 20),
        name="attend",
    )(q, k, v, clip_row)


def scatter_kernel(a_ref, w_ref, base_ref, hot_ref, gate_ref, out_ref, wbuf, part, got, land, outgo, fin,
                   wsem, dsend, drecv, nsend, nrecv, fsem):
    full = wbuf.shape[2]
    half = base_ref.shape[0] // 2
    feat = full // 2
    quarter = half // 2
    core = hid_place()[2]
    order = (Z2X, ZPX, ZMX, Z2, XP, ZP, ZM, OWN)

    w_copies = {}
    for role in order:
        cp = pltpu.make_async_copy(
            w_ref.at[:, pl.ds(pl.multiple_of(chip_of(role) * full, 128), full)], wbuf.at[role], wsem.at[role]
        )
        cp.start()
        w_copies[role] = cp

    barrier = pltpu.get_barrier_semaphore()
    pl.semaphore_signal(barrier, inc=1, device_id=hid_device(OWN, True), device_id_type=MESH)
    for role in (XP, ZM, ZP):
        pl.semaphore_signal(barrier, inc=1, device_id=hid_device(role, False), device_id_type=MESH)
    pl.semaphore_wait(barrier, 4)

    d_copies = {}

    def multiply(role):
        w_copies[role].wait()
        theirs = jnp.dot(a_ref[pl.ds((1 - core) * half, half)], wbuf[role], preferred_element_type=F32)
        outgo[role] = theirs.astype(BF16)
        cp = pltpu.make_async_remote_copy(
            outgo.at[role], got.at[role], dsend.at[role], drecv.at[role],
            device_id=hid_device(OWN, True), device_id_type=MESH,
        )
        cp.start()
        d_copies[role] = cp
        mine = jnp.dot(a_ref[pl.ds(core * half, half)], wbuf[role], preferred_element_type=F32)
        part[role] = mine.astype(BF16)

    sends = []
    def send(role, lo, count, to_role, slot, sem):
        cp = pltpu.make_async_remote_copy(
            part.at[role, pl.ds(lo, count)], land.at[slot, pl.ds(lo, count)], nsend.at[sem], nrecv.at[sem],
            device_id=hid_device(to_role, False), device_id_type=MESH,
        )
        cp.start()
        sends.append(cp)
        return cp

    def total(role, lo, count, slots):
        rows = pl.ds(lo, count)
        value = part[role, rows].astype(F32) + got[role, rows].astype(F32)
        for slot in slots:
            value = value + land[slot, rows].astype(F32)
        return value

    def fold(role, lo, count, slots):
        part[role, pl.ds(lo, count)] = total(role, lo, count, slots).astype(BF16)

    arrived = {}
    multiply(Z2X)
    multiply(ZPX)
    d_copies[Z2X].wait_recv()
    fold(Z2X, 0, half, ())
    arrived[0] = send(Z2X, 0, half, XP, 0, 0)
    multiply(ZMX)
    d_copies[ZPX].wait_recv()
    fold(ZPX, 0, half, ())
    arrived[1] = send(ZPX, 0, half, ZP, 1, 1)
    multiply(Z2)
    d_copies[ZMX].wait_recv()
    fold(ZMX, 0, half, ())
    arrived[2] = send(ZMX, 0, half, ZM, 2, 2)
    multiply(ZP)
    multiply(ZM)
    multiply(XP)
    d_copies[ZP].wait_recv()
    fold(ZP, quarter, quarter, ())
    arrived[8] = send(ZP, quarter, quarter, ZP, 5, 8)
    d_copies[ZM].wait_recv()
    fold(ZM, 0, quarter, ())
    arrived[9] = send(ZM, 0, quarter, ZM, 6, 9)
    multiply(OWN)
    d_copies[Z2].wait_recv()
    arrived[0].wait_recv()
    fold(Z2, 0, half, (0,))
    arrived[3] = send(Z2, 0, quarter, ZP, 3, 3)
    arrived[4] = send(Z2, quarter, quarter, ZM, 4, 4)
    d_copies[XP].wait_recv()
    arrived[1].wait_recv()
    arrived[2].wait_recv()
    fold(XP, 0, half, (1, 2))
    arrived[7] = send(XP, 0, half, XP, 7, 7)
    arrived[3].wait_recv()
    fold(ZP, 0, quarter, (3,))
    arrived[5] = send(ZP, 0, quarter, ZP, 5, 5)
    arrived[4].wait_recv()
    fold(ZM, quarter, quarter, (4,))
    arrived[6] = send(ZM, quarter, quarter, ZM, 6, 6)
    gates = jnp.dot(hot_ref[...], three_way(gate_ref[...]), preferred_element_type=F32)
    d_copies[OWN].wait_recv()
    for slot in (8, 9, 7, 5, 6):
        arrived[slot].wait_recv()
    summed = total(OWN, 0, half, (5, 6, 7))
    turned = pltpu.roll(summed, feat, 1)
    fin[0] = jnp.where(core == 0, turned, summed)[:, 0:feat]
    back = pltpu.make_async_remote_copy(
        fin.at[0], fin.at[1], fsem.at[0], fsem.at[1], device_id=hid_device(OWN, True), device_id_type=MESH
    )
    back.start()
    kept = jnp.where(core == 0, summed, turned)[:, 0:feat]
    for side in range(2):
        @pl.when(core == side)
        def _():
            here = pl.ds(side * half, half)
            out_ref[here] = (base_ref[here].astype(F32) + gates[side * half:(side + 1) * half] * kept).astype(BF16)
    back.wait()
    for side in range(2):
        @pl.when(core != side)
        def _():
            here = pl.ds(side * half, half)
            out_ref[here] = (base_ref[here].astype(F32) + gates[side * half:(side + 1) * half] * fin[1]).astype(BF16)
    for cp in sends:
        cp.wait_send()
    for role in order:
        d_copies[role].wait_send()


def project_scatter(a, w, base, hot, gate, cid):
    rows, depth = a.shape
    half, feat = rows // 2, base.shape[1]
    full = 2 * feat
    return pl.pallas_call(
        scatter_kernel,
        out_shape=jax.ShapeDtypeStruct(base.shape, BF16),
        in_specs=[VSPEC, ANYSPEC, VSPEC, VSPEC, VSPEC],
        out_specs=VSPEC,
        scratch_shapes=[
            pltpu.VMEM((8, depth, full), BF16),
            pltpu.VMEM((8, half, full), BF16),
            pltpu.VMEM((8, half, full), BF16),
            pltpu.VMEM((8, half, full), BF16),
            pltpu.VMEM((8, half, full), BF16),
            pltpu.VMEM((2, half, feat), F32),
            pltpu.SemaphoreType.DMA((8,)),
            pltpu.SemaphoreType.DMA((8,)),
            pltpu.SemaphoreType.DMA((8,)),
            pltpu.SemaphoreType.DMA((10,)),
            pltpu.SemaphoreType.DMA((10,)),
            pltpu.SemaphoreType.DMA((2,)),
        ],
        compiler_params=pltpu.CompilerParams(collective_id=cid, has_side_effects=True, vmem_limit_bytes=48 << 20),
        name="scatter_" + str(depth),
    )(a, w, base, hot, gate)


def shards(tokens, clip_id, clip_step, mod_table, w_query, w_key, w_value, q_gain, k_gain, w_out, w_up, w_down):
    feat = tokens.shape[1]
    mods = mod_table[clip_step].transpose(1, 0, 2)
    own = lax.dynamic_slice_in_dim(mods, lax.axis_index("hid") * feat, feat, 2)
    hot = (clip_id[:, None] == jnp.arange(24, dtype=jnp.int32)[None, :] % 8).astype(BF16)
    q, k, v = gather_project(
        "qkv", tokens, hot, jnp.stack([mods[1], mods[0]]), (w_query, w_key, w_value),
        (q_gain[None, :], k_gain[None, :]), 1,
    )
    attended = attend(q, k, v, clip_id.astype(F32)[None, :], 2)
    residual = project_scatter(attended, w_out, tokens, hot, own[2], 3)
    (hidden,) = gather_project("up", residual, hot, jnp.stack([mods[4], mods[3]]), (w_up,), (), 4)
    return project_scatter(hidden, w_down, residual, hot, own[5], 5)


def solution(mesh):
    placed = (
        P("seq", "hid"), P("seq"), P(), P(), P(None, "hid"), P(None, "hid"), P(None, "hid"), P("hid"), P("hid"),
        P("hid", None), P(None, "hid"), P("hid", None),
    )
    return jax.shard_map(shards, mesh=mesh, in_specs=placed, out_specs=P("seq", "hid"), check_vma=False)
```

```python
import functools
import jax
import jax.numpy as jnp
from jax import lax
from jax.experimental import pallas as pl
from jax.experimental.pallas import tpu as pltpu
from jax.sharding import PartitionSpec as P

MESH = pl.DeviceIdType.MESH
EPS = 1e-06
HEAD_DIM = 128
SCORE_SCALE = HEAD_DIM ** (-0.5) * 1.4426950408889634
FAR = -1e30
F32 = jnp.float32
BF16 = jnp.bfloat16
ANYSPEC = pl.BlockSpec(memory_space=pl.ANY)
VSPEC = pl.BlockSpec(memory_space=pltpu.VMEM)

OWN, XP, ZM, ZP, ZMX, ZPX, Z2, Z2X = range(8)
OFFSETS = ((0, 0), (0, 1), (3, 0), (1, 0), (3, 1), (1, 1), (2, 0), (2, 1))
BACK = (OWN, XP, ZP, ZM, ZPX, ZMX, Z2, Z2X)
Y_STEPS = (0, 3, 1, 2)
Y_BACK = (0, 2, 1, 3)
A, B = 0, 1


def hid_place():
    h = lax.axis_index("hid")
    return h // 4, lax.rem(h // 2, 2), lax.rem(h, 2)


def chip_of(role):
    z, x, _ = hid_place()
    dz, dx = OFFSETS[role]
    return lax.rem(z + dz, 4) * 2 + lax.rem(x + dx, 2)


def hid_device(role, flip):
    core = hid_place()[2]
    core = 1 - core if flip else core
    return {"hid": chip_of(role) * 2 + core}


def seq_device(y_role, flip):
    s = lax.axis_index("seq")
    y, x = s // 2, lax.rem(s, 2)
    x = 1 - x if flip else x
    return {"seq": lax.rem(y + Y_STEPS[y_role], 4) * 2 + x}


def pieces(values, count):
    parts = []
    for i in range(count - 1):
        piece = values.astype(BF16).astype(F32)
        parts.append(piece)
        values = values - piece
    return jnp.concatenate(parts + [values], axis=0).astype(BF16)


def rows_to_columns(rows, width):
    n = rows.shape[0]
    parts = pieces(rows, 3)
    pick = (
        lax.broadcasted_iota(jnp.int32, (3 * n, n * width), 1) // width
        == lax.rem(lax.broadcasted_iota(jnp.int32, (3 * n, n * width), 0), n)
    ).astype(F32).astype(BF16)
    return lax.dot_general(parts, pick, (((0,), (0,)), ((), ())), preferred_element_type=F32)


def lane_sums(values):
    ones = jnp.ones((8, values.shape[1]), BF16)
    dims = (((1,), (1,)), ((), ()))
    if values.dtype == BF16:
        return lax.dot_general(ones, values, dims, preferred_element_type=F32)[0:1]
    top = values.astype(BF16)
    rest = (values - top.astype(F32)).astype(BF16)
    both = lax.dot_general(ones, top, dims, preferred_element_type=F32)
    return (both + lax.dot_general(ones, rest, dims, preferred_element_type=F32))[0:1]


def greet(hid_all, hid_near, seq):
    barrier = pltpu.get_barrier_semaphore()
    peers = [hid_device(OWN, True)]
    if hid_all:
        peers += [hid_device(r, f) for r in range(1, 8) for f in (False, True)]
    elif hid_near:
        peers += [hid_device(r, False) for r in range(1, 8)]
    if seq:
        peers += [seq_device(y, f) for y in range(4) for f in (False, True) if (y, f) != (0, False)]
    for peer in peers:
        pl.semaphore_signal(barrier, inc=1, device_id=peer, device_id_type=MESH)
    pl.semaphore_wait(barrier, len(peers))


def remote(src, dst, send_sem, recv_sem, device):
    cp = pltpu.make_async_remote_copy(src, dst, send_sem, recv_sem, device_id=device, device_id_type=MESH)
    cp.start()
    return cp


def clip_one_hot(clip_row, width, period):
    ones = jnp.ones((1, width), BF16)
    cols = lax.dot_general(clip_row.astype(BF16), ones, (((0,), (0,)), ((), ())), preferred_element_type=F32)
    lane = lax.rem(lax.broadcasted_iota(jnp.int32, cols.shape, 1), period).astype(F32)
    return cols == lane


def load_columns_of_rows(w_refs, wbuf, wsem, widths):
    full = wbuf.shape[1]
    copies = {}
    for role in (OWN, ZM, ZP, XP, Z2, ZMX, ZPX, Z2X):
        at = 0
        for i, w_ref in enumerate(w_refs):
            cp = pltpu.make_async_copy(
                w_ref.at[pl.ds(chip_of(role) * full, full)], wbuf.at[role, :, pl.ds(at, widths[i])], wsem.at[role, i]
            )
            cp.start()
            copies[role, i] = cp
            at += widths[i]
    return copies


SCATTER_ORDER = (Z2X, ZPX, ZMX, Z2, ZP, ZM, XP, OWN)


def load_blocks_of_columns(w_ref, wbuf, wsem):
    full = wbuf.shape[2]
    copies = {}
    for role in SCATTER_ORDER:
        cp = pltpu.make_async_copy(
            w_ref.at[:, pl.ds(pl.multiple_of(chip_of(role) * full, 128), full)], wbuf.at[role], wsem.at[role]
        )
        cp.start()
        copies[role] = cp
    return copies


def gather_phase(x_ref, hot_ref, mod_ref, scale_at, w_copies, n_weights, width,
                 raw, nrm, pair, stat, wbuf, acc, psem, ssend, srecv, rsend, rrecv, dsend, drecv):
    half, full = raw.shape[1], raw.shape[2]
    part = full // 2
    quarter = half // 2
    core = hid_place()[2]
    swap = remote(
        x_ref.at[pl.ds((1 - core) * half, half)], pair, psem.at[0], psem.at[1], hid_device(OWN, True)
    )

    def place(shift):
        rows = lax.broadcasted_iota(jnp.int32, (part, full), 0)
        cols = lax.broadcasted_iota(jnp.int32, (part, full), 1)
        return (cols == rows + shift).astype(F32).astype(BF16)

    mine = jnp.dot(x_ref[pl.ds(core * half, half)], place(core * part), preferred_element_type=F32)
    swap.wait_recv()
    block = mine + jnp.dot(pair[...], place((1 - core) * part), preferred_element_type=F32)
    raw[OWN] = block.astype(BF16)
    sends = {}

    def send_raw(slot, which, to_role, to_slot):
        rows = pl.ds(which * quarter, quarter)
        sends[to_slot, which] = remote(
            raw.at[slot, rows], raw.at[to_slot, rows], rsend.at[to_slot, which], rrecv.at[to_slot, which],
            hid_device(to_role, False),
        )

    def await_raw(slot, which):
        sends[slot, which].wait_recv()

    send_raw(OWN, A, ZP, ZM)
    send_raw(OWN, B, ZM, ZP)
    send_raw(OWN, A, XP, XP)
    stat[OWN, 0:1] = lane_sums(raw[OWN])
    stat[OWN, 1:2] = lane_sums(block * block)
    stat_copies = [
        remote(stat.at[OWN], stat.at[BACK[r]], ssend.at[r], srecv.at[BACK[r]], hid_device(r, False))
        for r in range(1, 8)
    ]
    send_raw(OWN, B, ZP, ZM)
    send_raw(OWN, A, ZM, ZP)
    send_raw(OWN, B, XP, XP)
    d_copies = {}
    hot = [hot_ref[pl.ds(pl.multiple_of(core * half + i * quarter, quarter), quarter)] for i in range(2)]
    for cp in stat_copies:
        cp.wait_recv()
    totals = stat[0]
    for r in range(1, 8):
        totals = totals + stat[r]
    moments = rows_to_columns(totals * (1.0 / (full * 8)), 128)
    row_mean = moments[:, 0:1]
    inv = lax.rsqrt(moments[:, 128:129] - row_mean * row_mean + EPS)

    def normalize(role, which):
        col = pl.multiple_of(chip_of(role) * full, 128)
        rows = slice(which * quarter, (which + 1) * quarter)
        scale = jnp.dot(hot[which], pieces(mod_ref[scale_at, :, pl.ds(col, full)], 3), preferred_element_type=F32)
        shift = jnp.dot(hot[which], pieces(mod_ref[scale_at - 1, :, pl.ds(col, full)], 3), preferred_element_type=F32)
        values = (raw[role, rows].astype(F32) - row_mean[rows]) * inv[rows]
        nrm[core, role, rows] = (values * (1.0 + scale) + shift).astype(BF16)
        d_copies[role, which] = remote(
            nrm.at[core, role, rows], nrm.at[core, role, rows], dsend.at[role, which], drecv.at[role, which],
            hid_device(OWN, True),
        )

    first = [True, True]

    def multiply(role, theirs):
        side = 1 - core if theirs else core
        if theirs:
            d_copies[role, A].wait_recv()
            d_copies[role, B].wait_recv()
        else:
            for i in range(n_weights):
                w_copies[role, i].wait()
        term = jnp.dot(nrm[side, role], wbuf[role, :, 0:width], preferred_element_type=F32)
        if first[theirs]:
            acc[side, :, 0:width] = term
        else:
            acc[side, :, 0:width] += term
        first[theirs] = False

    normalize(OWN, A)
    normalize(OWN, B)
    await_raw(ZM, A)
    send_raw(ZM, A, ZP, Z2)
    await_raw(ZP, B)
    send_raw(ZP, B, ZM, Z2)
    await_raw(XP, A)
    send_raw(XP, A, ZP, ZMX)
    send_raw(XP, A, ZM, ZPX)
    multiply(OWN, False)
    normalize(ZM, A)
    normalize(ZP, B)
    normalize(XP, A)
    multiply(OWN, True)
    await_raw(XP, B)
    send_raw(XP, B, ZP, ZMX)
    send_raw(XP, B, ZM, ZPX)
    normalize(XP, B)
    await_raw(ZM, B)
    normalize(ZM, B)
    multiply(XP, False)
    await_raw(ZP, A)
    normalize(ZP, A)
    multiply(ZM, False)
    multiply(ZP, False)
    multiply(XP, True)
    await_raw(Z2, A)
    send_raw(Z2, A, XP, Z2X)
    await_raw(Z2, B)
    send_raw(Z2, B, XP, Z2X)
    normalize(Z2, A)
    normalize(Z2, B)
    multiply(ZM, True)
    multiply(ZP, True)
    multiply(Z2, False)
    multiply(Z2, True)
    await_raw(ZMX, A)
    normalize(ZMX, A)
    await_raw(ZPX, A)
    normalize(ZPX, A)
    await_raw(Z2X, A)
    normalize(Z2X, A)
    await_raw(ZMX, B)
    normalize(ZMX, B)
    await_raw(ZPX, B)
    normalize(ZPX, B)
    multiply(ZMX, False)
    await_raw(Z2X, B)
    normalize(Z2X, B)
    multiply(ZPX, False)
    multiply(Z2X, False)
    multiply(ZMX, True)
    multiply(ZPX, True)
    multiply(Z2X, True)
    swap.wait_send()
    for cp in stat_copies + list(sends.values()) + list(d_copies.values()):
        cp.wait_send()


def head_norm_phase(acc, gains, outs, qstat, qsend, qrecv):
    half = acc.shape[1]
    wq = outs[0].shape[1]
    for side in range(2):
        for i in range(2):
            values = acc[side, :, i * wq:(i + 1) * wq]
            qstat[0, 2 * side + i:2 * side + i + 1] = lane_sums(values * values)
    copies = []
    for flip in (False, True):
        for role in range(8):
            if role == OWN and not flip:
                continue
            there = BACK[role] + 8 * flip
            copies.append(
                remote(qstat.at[0], qstat.at[there], qsend.at[role + 8 * flip], qrecv.at[there], hid_device(role, flip))
            )
    for side in range(2):
        outs[2][pl.ds(side * half, half)] = acc[side, :, 2 * wq:3 * wq].astype(BF16)
    for cp in copies:
        cp.wait_recv()
    sums = qstat[0]
    for i in range(1, 16):
        sums = sums + qstat[i]
    scales = lax.rsqrt(rows_to_columns(sums * (1.0 / (16 * wq)), 128) + EPS)
    for side in range(2):
        for i in range(2):
            at = (2 * side + i) * 128
            by = scales[:, at:at + 1] * (SCORE_SCALE if i == 0 else 1.0)
            outs[i][pl.ds(side * half, half)] = (acc[side, :, i * wq:(i + 1) * wq] * by * gains[i][...]).astype(BF16)
    for cp in copies:
        cp.wait_send()


def attend_phase(q_ref, k_ref, v_ref, clip_ref, out_ref, qb, kb, vb, crow, best, acc, obuf,
                 xsend, xrecv, ysend, yrecv, csend, crecv, osem, meanwhile=None):
    rows = q_ref.shape[0]
    tile = rows // 2
    xh = lax.rem(lax.axis_index("seq"), 2)
    mine = pl.ds(pl.multiple_of(xh * HEAD_DIM, HEAD_DIM), HEAD_DIM)
    other = pl.ds(pl.multiple_of((1 - xh) * HEAD_DIM, HEAD_DIM), HEAD_DIM)
    low = pl.ds(0, HEAD_DIM)
    peers = [(y, f) for y in range(4) for f in (0, 1) if (y, f) != (0, 0)]
    started = []

    def send(src, dst, send_sem, recv_sem, y, f):
        started.append(remote(src, dst, send_sem, recv_sem, seq_device(y, f)))
        return started[-1]

    crow[0] = clip_ref[...]
    clips = [
        send(crow.at[0], crow.at[Y_BACK[y] * 2 + f], csend.at[y * 2 + f], crecv.at[Y_BACK[y] * 2 + f], y, f)
        for y, f in peers
    ]
    kb[0, :, 0:HEAD_DIM] = k_ref[:, mine]
    vb[0, :, 0:HEAD_DIM] = v_ref[:, mine]

    def send_y(buf, which, slot, y_role, to_slot):
        return send(
            buf.at[slot, :, low], buf.at[to_slot, :, low],
            ysend.at[which, to_slot], yrecv.at[which, to_slot], y_role, 0,
        )

    ys = {}
    ys["k", 2] = send_y(kb, 0, 0, 2, 2)
    ys["v", 4] = send_y(vb, 1, 0, 1, 4)
    x_k = send(k_ref.at[:, other], kb.at[1, :, low], xsend.at[0], xrecv.at[0], 0, 1)
    ys["v", 2] = send_y(vb, 1, 0, 2, 2)
    ys["k", 4] = send_y(kb, 0, 0, 1, 4)
    x_v = send(v_ref.at[:, other], vb.at[1, :, low], xsend.at[1], xrecv.at[1], 0, 1)
    x_q = send(q_ref.at[:, other], qb.at[pl.ds(rows, rows), low], xsend.at[2], xrecv.at[2], 0, 1)
    if meanwhile:
        meanwhile()

    def mark_keys(slot):
        kb[slot, :, HEAD_DIM:2 * HEAD_DIM] = jnp.where(clip_one_hot(crow[slot], HEAD_DIM, HEAD_DIM), 0.0, FAR).astype(BF16)

    def mark_queries(side):
        qb[pl.ds(side * rows, rows), HEAD_DIM:2 * HEAD_DIM] = (
            clip_one_hot(crow[side], HEAD_DIM, HEAD_DIM).astype(F32).astype(BF16)
        )

    def attend_pair(slot, side):
        ats = [pl.ds(pl.multiple_of(side * rows + i * tile, tile), tile) for i in range(2)]
        scores = [
            lax.dot_general(qb[at], kb[slot], (((1,), (1,)), ((), ())), preferred_element_type=F32) for at in ats
        ]
        olds = [best[at] for at in ats]
        before = [acc[at] for at in ats]
        done = []
        for i in range(2):
            old = olds[i][:, 0:1]
            fresh = jnp.maximum(old, jnp.max(scores[i], axis=1, keepdims=True))
            weights = jnp.exp2(scores[i] - fresh).astype(BF16)
            mixed = jnp.dot(weights, vb[slot], preferred_element_type=F32)
            done.append((fresh, before[i] * jnp.exp2(old - fresh) + mixed))
        for i in range(2):
            best[ats[i]] = jnp.broadcast_to(done[i][0], (tile, HEAD_DIM))
            acc[ats[i]] = done[i][1]

    def attend_many(count, pick):
        def step(i, carry):
            attend_pair(*pick(i))
            return carry

        lax.fori_loop(0, count, step, 0)

    qb[pl.ds(0, rows), 0:HEAD_DIM] = q_ref[:, mine]
    best[...] = jnp.full(best.shape, 3.0 * FAR, F32)
    acc[...] = jnp.zeros_like(acc)
    for slot in range(8):
        vb[slot, :, HEAD_DIM:2 * HEAD_DIM] = jnp.ones((rows, HEAD_DIM), BF16)
    mark_keys(0)
    mark_queries(0)
    attend_pair(0, 0)
    for cp in clips:
        cp.wait_recv()
    mark_queries(1)
    for slot in range(1, 8):
        mark_keys(slot)
    ys["k", 2].wait_recv()
    ys["k", 6] = send_y(kb, 0, 2, 2, 6)
    ys["v", 4].wait_recv()
    ys["v", 6] = send_y(vb, 1, 4, 1, 6)
    x_k.wait_recv()
    ys["k", 3] = send_y(kb, 0, 1, 2, 3)
    x_v.wait_recv()
    ys["v", 5] = send_y(vb, 1, 1, 1, 5)
    ys["v", 3] = send_y(vb, 1, 1, 2, 3)
    ys["k", 5] = send_y(kb, 0, 1, 1, 5)
    attend_pair(1, 0)
    ys["v", 2].wait_recv()
    attend_pair(2, 0)
    ys["k", 4].wait_recv()
    attend_pair(4, 0)
    x_q.wait_recv()
    attend_many(2, lambda i: (i, 1))
    attend_many(2, lambda i: (2 * i + 2, 1))
    ys["k", 3].wait_recv()
    ys["k", 7] = send_y(kb, 0, 3, 2, 7)
    ys["v", 5].wait_recv()
    ys["v", 7] = send_y(vb, 1, 5, 1, 7)
    ys["k", 6].wait_recv()
    ys["v", 6].wait_recv()
    attend_many(2, lambda i: (6, i))
    ys["v", 3].wait_recv()
    ys["k", 5].wait_recv()
    attend_many(4, lambda i: (3 + i // 2 * 2, lax.rem(i, 2)))
    ys["k", 7].wait_recv()
    ys["v", 7].wait_recv()
    attend_pair(7, 1)

    def finished(side):
        at = pl.ds(side * rows, rows)
        return (acc[at, 0:HEAD_DIM] / acc[at, HEAD_DIM:2 * HEAD_DIM]).astype(BF16)

    obuf[...] = finished(1)
    back = send(obuf, out_ref.at[:, mine], osem.at[0], osem.at[1], 0, 1)
    attend_pair(7, 0)
    out_ref[:, mine] = finished(0)
    back.wait_recv()
    for cp in started:
        cp.wait_send()


def scatter_phase(a_ref, w_copies, base_ref, hot_ref, mod_ref, gate_at, out_ref, wbuf,
                  part, got, land, outgo, fin, dsend, drecv, nsend, nrecv, fsem):
    depth, full = wbuf.shape[1], wbuf.shape[2]
    half = part.shape[1]
    feat = full // 2
    quarter = half // 2
    core = hid_place()[2]
    d_copies = {}
    sends = []
    arrived = {}

    def multiply(role):
        w_copies[role].wait()
        theirs = jnp.dot(a_ref[pl.ds((1 - core) * half, half), 0:depth], wbuf[role], preferred_element_type=F32)
        outgo[role] = theirs.astype(BF16)
        d_copies[role] = remote(
            outgo.at[role], got.at[role], dsend.at[role], drecv.at[role], hid_device(OWN, True)
        )
        mine = jnp.dot(a_ref[pl.ds(core * half, half), 0:depth], wbuf[role], preferred_element_type=F32)
        part[role] = mine.astype(BF16)

    def send(role, which, to_role, slot):
        rows = pl.ds(which * quarter, quarter)
        arrived[slot, which] = remote(
            part.at[role, rows], land.at[slot, rows], nsend.at[slot, which], nrecv.at[slot, which],
            hid_device(to_role, False),
        )

    def total(role, which, slots):
        rows = slice(which * quarter, (which + 1) * quarter)
        value = part[role, rows].astype(F32) + got[role, rows].astype(F32)
        for slot in slots:
            arrived[slot, which].wait_recv()
            value = value + land[slot, rows].astype(F32)
        return value

    def fold(role, which, slots=()):
        part[role, which * quarter:(which + 1) * quarter] = total(role, which, slots).astype(BF16)

    multiply(Z2X)
    multiply(ZPX)
    multiply(ZMX)
    d_copies[Z2X].wait_recv()
    fold(Z2X, A)
    send(Z2X, A, XP, 0)
    fold(Z2X, B)
    send(Z2X, B, XP, 0)
    d_copies[ZPX].wait_recv()
    fold(ZPX, A)
    send(ZPX, A, ZP, 1)
    d_copies[ZMX].wait_recv()
    fold(ZMX, A)
    send(ZMX, A, ZM, 2)
    fold(ZPX, B)
    send(ZPX, B, ZP, 1)
    fold(ZMX, B)
    send(ZMX, B, ZM, 2)
    multiply(Z2)
    multiply(ZP)
    multiply(ZM)
    d_copies[Z2].wait_recv()
    fold(Z2, A, (0,))
    send(Z2, A, ZP, 3)
    multiply(XP)
    d_copies[ZP].wait_recv()
    fold(ZP, B)
    d_copies[ZM].wait_recv()
    fold(ZM, A)
    d_copies[XP].wait_recv()
    fold(XP, A, (1, 2))
    send(XP, A, XP, 7)
    fold(Z2, B, (0,))
    send(Z2, B, ZM, 4)
    send(ZP, B, ZP, 5)
    send(ZM, A, ZM, 6)
    multiply(OWN)
    fold(XP, B, (1, 2))
    send(XP, B, XP, 7)
    fold(ZP, A, (3,))
    send(ZP, A, ZP, 5)
    fold(ZM, B, (4,))
    send(ZM, B, ZM, 6)
    col = pl.multiple_of(chip_of(OWN) * full, 128)
    gates = jnp.dot(hot_ref[...], pieces(mod_ref[gate_at, :, pl.ds(col, full)], 3), preferred_element_type=F32)
    gates = jnp.where(core == 0, gates, pltpu.roll(gates, feat, 1))[:, 0:feat]
    d_copies[OWN].wait_recv()
    kept = []
    backs = []
    for which in (A, B):
        rows = pl.ds(which * quarter, quarter)
        summed = total(OWN, which, (7, 5, 6) if which == B else (7, 6, 5))
        turned = pltpu.roll(summed, feat, 1)
        fin[0, rows] = jnp.where(core == 0, turned, summed)[:, 0:feat]
        backs.append(remote(fin.at[0, rows], fin.at[1, rows], fsem.at[0, which], fsem.at[1, which], hid_device(OWN, True)))
        kept.append(jnp.where(core == 0, summed, turned)[:, 0:feat])

    def finish(mine):
        for side in range(2):
            @pl.when((core == side) if mine else (core != side))
            def _():
                for which in (A, B):
                    lo = side * half + which * quarter
                    terms = kept[which] if mine else fin[1, which * quarter:(which + 1) * quarter]
                    out_ref[lo:lo + quarter] = (
                        base_ref[lo:lo + quarter].astype(F32) + gates[lo:lo + quarter] * terms
                    ).astype(BF16)

    finish(True)
    for cp in backs:
        cp.wait_recv()
    finish(False)
    for cp in backs + list(arrived.values()) + list(d_copies.values()):
        cp.wait_send()


GATHER_SEMS = [(2,), (8,), (8,), (8, 2), (8, 2), (8, 2), (8, 2)]
ATTEND_SEMS = [(3,), (3,), (2, 8), (2, 8), (8,), (8,), (2,)]
SCATTER_SEMS = [(8,), (8,), (8, 2), (8, 2), (2, 2)]


def sems(shapes):
    return [pltpu.SemaphoreType.DMA(s) for s in shapes]


def gather_scratch(half, full, width):
    return [
        pltpu.VMEM((8, half, full), BF16),
        pltpu.VMEM((2, 8, half, full), BF16),
        pltpu.VMEM((half, full // 2), BF16),
        pltpu.VMEM((8, 2, half), F32),
        pltpu.VMEM((8, full, width), BF16),
        pltpu.VMEM((2, half, width), F32),
    ]


def attend_scratch(rows):
    return [
        pltpu.VMEM((2 * rows, 2 * HEAD_DIM), BF16),
        pltpu.VMEM((8, rows, 2 * HEAD_DIM), BF16),
        pltpu.VMEM((8, rows, 2 * HEAD_DIM), BF16),
        pltpu.VMEM((8, 1, rows), F32),
        pltpu.VMEM((2 * rows, HEAD_DIM), F32),
        pltpu.VMEM((2 * rows, 2 * HEAD_DIM), F32),
        pltpu.VMEM((rows, HEAD_DIM), BF16),
    ]


def scatter_scratch(half, full):
    return [pltpu.VMEM((8, half, full), BF16)] * 4 + [pltpu.VMEM((2, half, full // 2), F32)]


def block_kernel(tokens, clip_ref, mod_ref, w_query, w_key, w_value, q_gain, k_gain, w_out, w_up, w_down, out_ref,
                 x, hot, q, k, v, attended, residual, hidden, qstat, w_first, w_mix, w_last, acc, *refs):
    (x_sem, w_sem, up_sem, mix_sem, last_sem, qs_sem, qr_sem), refs = refs[:7], refs[7:]
    gather_bufs, refs = refs[:4], refs[4:]
    attend_bufs, refs = refs[:7], refs[7:]
    scatter_bufs, refs = refs[:5], refs[5:]
    gather_sems, attend_sems, scatter_sems = refs[:7], refs[7:14], refs[14:]
    half = acc.shape[1]
    width = w_query.shape[1]
    wide = w_up.shape[1]

    x_copy = pltpu.make_async_copy(tokens, x, x_sem.at[0])
    x_copy.start()
    first = load_columns_of_rows((w_query, w_key, w_value), w_first, w_sem, (width,) * 3)
    hot[...] = clip_one_hot(clip_ref[...], 24, 8).astype(F32).astype(BF16)
    x_copy.wait()
    greet(True, True, True)
    gather_phase(x, hot, mod_ref, 1, first, 3, 3 * width, *gather_bufs, w_first, acc, *gather_sems)
    head_norm_phase(acc, (q_gain, k_gain), (q, k, v), qstat, qs_sem, qr_sem)
    later = {}

    def load_later():
        later["mix"] = load_blocks_of_columns(w_out, w_mix, mix_sem)
        later["up"] = load_columns_of_rows((w_up,), w_first, up_sem, (wide,))
        later["last"] = load_blocks_of_columns(w_down, w_last, last_sem)

    attend_phase(q, k, v, clip_ref, attended, *attend_bufs, *attend_sems, meanwhile=load_later)
    scatter_phase(attended, later["mix"], x, hot, mod_ref, 2, residual, w_mix, *scatter_bufs, *scatter_sems)
    gather_phase(residual, hot, mod_ref, 4, later["up"], 1, wide, *gather_bufs, w_first, acc, *gather_sems)
    for side in range(2):
        hidden[pl.ds(side * half, half)] = jax.nn.gelu(acc[side, :, 0:wide], approximate=True).astype(BF16)
    scatter_phase(hidden, later["last"], residual, hot, mod_ref, 5, out_ref, w_last, *scatter_bufs, *scatter_sems)


def block(tokens, clip_row, mods, w_query, w_key, w_value, q_gain, k_gain, w_out, w_up, w_down):
    rows, part = tokens.shape
    half, full = rows // 2, 2 * part
    width, wide = w_query.shape[1], w_up.shape[1]
    gather = gather_scratch(half, full, 3 * width)
    scratch = [
        pltpu.VMEM((rows, part), BF16),
        pltpu.VMEM((rows, 24), BF16),
        pltpu.VMEM((rows, width), BF16),
        pltpu.VMEM((rows, width), BF16),
        pltpu.VMEM((rows, width), BF16),
        pltpu.VMEM((rows, width), BF16),
        pltpu.VMEM((rows, part), BF16),
        pltpu.VMEM((rows, wide), BF16),
        pltpu.VMEM((16, 4, half), F32),
        gather[4],
        pltpu.VMEM((8, width, full), BF16),
        pltpu.VMEM((8, wide, full), BF16),
        gather[5],
    ]
    scratch += sems([(1,), (8, 3), (8, 1), (8,), (8,), (16,), (16,)])
    scratch += gather[:4] + attend_scratch(rows) + scatter_scratch(half, full)
    scratch += sems(GATHER_SEMS + ATTEND_SEMS + SCATTER_SEMS)
    return pl.pallas_call(
        block_kernel,
        out_shape=jax.ShapeDtypeStruct((rows, part), BF16),
        in_specs=[ANYSPEC, VSPEC, VSPEC, ANYSPEC, ANYSPEC, ANYSPEC, VSPEC, VSPEC, ANYSPEC, ANYSPEC, ANYSPEC],
        out_specs=VSPEC,
        scratch_shapes=scratch,
        compiler_params=pltpu.CompilerParams(collective_id=1, has_side_effects=True, vmem_limit_bytes=60 << 20),
        name="block",
    )(tokens, clip_row, mods, w_query, w_key, w_value, q_gain, k_gain, w_out, w_up, w_down)


def shards(tokens, clip_id, clip_step, mod_table, w_query, w_key, w_value, q_gain, k_gain, w_out, w_up, w_down):
    mods = mod_table[clip_step].transpose(1, 0, 2)
    return block(
        tokens, clip_id.astype(F32)[None, :], mods, w_query, w_key, w_value, q_gain[None, :], k_gain[None, :],
        w_out, w_up, w_down,
    )


def solution(mesh):
    placed = (
        P("seq", "hid"), P("seq"), P(), P(), P(None, "hid"), P(None, "hid"), P(None, "hid"), P("hid"), P("hid"),
        P("hid", None), P(None, "hid"), P("hid", None),
    )
    return jax.shard_map(shards, mesh=mesh, in_specs=placed, out_specs=P("seq", "hid"), check_vma=False)
```

```python
import functools
import jax
import jax.numpy as jnp
from jax import lax
from jax.experimental import pallas as pl
from jax.experimental.pallas import tpu as pltpu
from jax.sharding import PartitionSpec as P

MESH = pl.DeviceIdType.MESH
EPS = 1e-06
HEAD_DIM = 128
SCORE_SCALE = HEAD_DIM ** (-0.5) * 1.4426950408889634
FAR = -1e30
F32 = jnp.float32
BF16 = jnp.bfloat16
ANYSPEC = pl.BlockSpec(memory_space=pl.ANY)
VSPEC = pl.BlockSpec(memory_space=pltpu.VMEM)

OWN, XP, ZM, ZP, ZMX, ZPX, Z2, Z2X = range(8)
OFFSETS = ((0, 0), (0, 1), (3, 0), (1, 0), (3, 1), (1, 1), (2, 0), (2, 1))
BACK = (OWN, XP, ZP, ZM, ZPX, ZMX, Z2, Z2X)
Y_STEPS = (0, 3, 1, 2)
Y_BACK = (0, 2, 1, 3)
A, B = 0, 1


def hid_place():
    h = lax.axis_index("hid")
    return h // 4, lax.rem(h // 2, 2), lax.rem(h, 2)


def chip_of(role):
    z, x, _ = hid_place()
    dz, dx = OFFSETS[role]
    return lax.rem(z + dz, 4) * 2 + lax.rem(x + dx, 2)


def hid_device(role, flip):
    core = hid_place()[2]
    core = 1 - core if flip else core
    return {"hid": chip_of(role) * 2 + core}


def seq_device(y_role, flip):
    s = lax.axis_index("seq")
    y, x = s // 2, lax.rem(s, 2)
    x = 1 - x if flip else x
    return {"seq": lax.rem(y + Y_STEPS[y_role], 4) * 2 + x}


def pieces(values, count):
    parts = []
    for i in range(count - 1):
        piece = values.astype(BF16).astype(F32)
        parts.append(piece)
        values = values - piece
    return jnp.concatenate(parts + [values], axis=0).astype(BF16)


def rows_to_columns(rows, width):
    n = rows.shape[0]
    parts = pieces(rows, 3)
    pick = (
        lax.broadcasted_iota(jnp.int32, (3 * n, n * width), 1) // width
        == lax.rem(lax.broadcasted_iota(jnp.int32, (3 * n, n * width), 0), n)
    ).astype(F32).astype(BF16)
    return lax.dot_general(parts, pick, (((0,), (0,)), ((), ())), preferred_element_type=F32)


def identity(size):
    rows = lax.broadcasted_iota(jnp.int32, (size, size), 0)
    return (rows == lax.broadcasted_iota(jnp.int32, (size, size), 1)).astype(F32).astype(BF16)


def lane_sums(values):
    ones = jnp.ones((8, values.shape[1]), BF16)
    dims = (((1,), (1,)), ((), ()))
    if values.dtype == BF16:
        return lax.dot_general(ones, values, dims, preferred_element_type=F32)[0:1]
    top = values.astype(BF16)
    rest = (values - top.astype(F32)).astype(BF16)
    both = lax.dot_general(ones, top, dims, preferred_element_type=F32)
    return (both + lax.dot_general(ones, rest, dims, preferred_element_type=F32))[0:1]


def greet(hid_all, hid_near, seq):
    barrier = pltpu.get_barrier_semaphore()
    peers = [hid_device(OWN, True)]
    if hid_all:
        peers += [hid_device(r, f) for r in range(1, 8) for f in (False, True)]
    elif hid_near:
        peers += [hid_device(r, False) for r in range(1, 8)]
    if seq:
        peers += [seq_device(y, f) for y in range(4) for f in (False, True) if (y, f) != (0, False)]
    for peer in peers:
        pl.semaphore_signal(barrier, inc=1, device_id=peer, device_id_type=MESH)
    pl.semaphore_wait(barrier, len(peers))


def remote(src, dst, send_sem, recv_sem, device):
    cp = pltpu.make_async_remote_copy(src, dst, send_sem, recv_sem, device_id=device, device_id_type=MESH)
    cp.start()
    return cp


def clip_one_hot(clip_row, width, period):
    ones = jnp.ones((1, width), BF16)
    cols = lax.dot_general(clip_row.astype(BF16), ones, (((0,), (0,)), ((), ())), preferred_element_type=F32)
    lane = lax.rem(lax.broadcasted_iota(jnp.int32, cols.shape, 1), period).astype(F32)
    return cols == lane


def load_columns_of_rows(w_refs, wbuf, wsem, widths):
    full = wbuf.shape[1]
    copies = {}
    for role in (OWN, ZM, ZP, XP, Z2, ZMX, ZPX, Z2X):
        at = 0
        for i, w_ref in enumerate(w_refs):
            cp = pltpu.make_async_copy(
                w_ref.at[pl.ds(chip_of(role) * full, full)], wbuf.at[role, :, pl.ds(at, widths[i])], wsem.at[role, i]
            )
            cp.start()
            copies[role, i] = cp
            at += widths[i]
    return copies


SCATTER_ORDER = (Z2X, ZPX, ZMX, Z2, ZP, ZM, XP, OWN)


def load_blocks_of_columns(w_ref, wbuf, wsem):
    full = wbuf.shape[2]
    copies = {}
    for role in SCATTER_ORDER:
        cp = pltpu.make_async_copy(
            w_ref.at[:, pl.ds(pl.multiple_of(chip_of(role) * full, 128), full)], wbuf.at[role], wsem.at[role]
        )
        cp.start()
        copies[role] = cp
    return copies


def pair_rows(x_ref, raw, pair, psem):
    half, full = raw.shape[1], raw.shape[2]
    part = full // 2
    core = hid_place()[2]
    swap = remote(
        x_ref.at[pl.ds((1 - core) * half, half)], pair, psem.at[0], psem.at[1], hid_device(OWN, True)
    )

    def place(shift):
        rows = lax.broadcasted_iota(jnp.int32, (part, full), 0)
        cols = lax.broadcasted_iota(jnp.int32, (part, full), 1)
        return (cols == rows + shift).astype(F32).astype(BF16)

    mine = jnp.dot(x_ref[pl.ds(core * half, half)], place(core * part), preferred_element_type=F32)
    swap.wait_recv()
    block = mine + jnp.dot(pair[...], place((1 - core) * part), preferred_element_type=F32)
    raw[OWN] = block.astype(BF16)
    swap.wait_send()


def gather_phase(hot_ref, mod_ref, scale_at, w_copies, n_weights, width,
                 raw, nrm, stat, norm, wbuf, acc, ssend, srecv, rsend, rrecv, dsend, drecv, meanwhile=None, free=None):
    half, full = raw.shape[1], raw.shape[2]
    quarter = half // 2
    core = hid_place()[2]
    sends = {}

    def send_raw(slot, which, to_role, to_slot):
        rows = pl.ds(which * quarter, quarter)
        sends[to_slot, which] = remote(
            raw.at[slot, rows], raw.at[to_slot, rows], rsend.at[to_slot, which], rrecv.at[to_slot, which],
            hid_device(to_role, False),
        )

    def await_raw(slot, which):
        sends[slot, which].wait_recv()

    send_raw(OWN, A, ZP, ZM)
    send_raw(OWN, B, ZM, ZP)
    send_raw(OWN, A, XP, XP)
    block = raw[OWN].astype(F32)
    stat[OWN, 0:1] = lane_sums(raw[OWN])
    stat[OWN, 1:2] = lane_sums(block * block)
    stat_copies = [
        remote(stat.at[OWN], stat.at[BACK[r]], ssend.at[r], srecv.at[BACK[r]], hid_device(r, False))
        for r in range(1, 8)
    ]
    send_raw(OWN, B, ZP, ZM)
    send_raw(OWN, A, ZM, ZP)
    send_raw(OWN, B, XP, XP)
    d_copies = {}
    hot = [hot_ref[pl.ds(pl.multiple_of(core * half + i * quarter, quarter), quarter)] for i in range(2)]
    for cp in stat_copies:
        cp.wait_recv()
    totals = stat[0]
    for r in range(1, 8):
        totals = totals + stat[r]
    moments = rows_to_columns(totals * (1.0 / (full * 8)), 128)
    norm[0] = moments[:, 0:128]
    norm[1] = lax.rsqrt(moments[:, 128:256] - moments[:, 0:128] * moments[:, 0:128] + EPS)

    def normalize(role, which):
        col = chip_of(role) * full
        rows = pl.ds(which * quarter, quarter)

        def lane_tile(n, carry):
            here = pl.ds(pl.multiple_of(n * 128, 128), 128)
            there = pl.ds(pl.multiple_of(col + n * 128, 128), 128)
            scale = jnp.dot(hot[which], pieces(mod_ref[scale_at, :, there], 3), preferred_element_type=F32)
            shift = jnp.dot(hot[which], pieces(mod_ref[scale_at - 1, :, there], 3), preferred_element_type=F32)
            values = (raw[role, rows, here].astype(F32) - norm[0, rows]) * norm[1, rows]
            nrm[core, role, rows, here] = (values * (1.0 + scale) + shift).astype(BF16)
            return carry

        lax.fori_loop(0, full // 128, lane_tile, 0)
        d_copies[role, which] = remote(
            nrm.at[core, role, rows], nrm.at[core, role, rows], dsend.at[role, which], drecv.at[role, which],
            hid_device(OWN, True),
        )

    first = [True, True]

    def multiply(role, theirs):
        side = 1 - core if theirs else core
        if theirs:
            d_copies[role, A].wait_recv()
            d_copies[role, B].wait_recv()
        else:
            for i in range(n_weights):
                w_copies[role, i].wait()
        fresh = first[theirs]
        first[theirs] = False

        def column_tile(n, carry):
            cols = pl.ds(pl.multiple_of(n * 256, 256), 256)
            term = jnp.dot(nrm[side, role], wbuf[role, :, cols], preferred_element_type=F32)
            if fresh:
                acc[side, :, cols] = term
            else:
                acc[side, :, cols] += term
            return carry

        lax.fori_loop(0, width // 256, column_tile, 0)

    if free is not None:
        pl.semaphore_wait(free, 1)
    normalize(OWN, A)
    normalize(OWN, B)
    await_raw(ZM, A)
    send_raw(ZM, A, ZP, Z2)
    await_raw(ZP, B)
    send_raw(ZP, B, ZM, Z2)
    await_raw(XP, A)
    send_raw(XP, A, ZP, ZMX)
    send_raw(XP, A, ZM, ZPX)
    multiply(OWN, False)
    normalize(ZM, A)
    normalize(ZP, B)
    normalize(XP, A)
    multiply(OWN, True)
    await_raw(XP, B)
    send_raw(XP, B, ZP, ZMX)
    send_raw(XP, B, ZM, ZPX)
    normalize(XP, B)
    await_raw(ZM, B)
    normalize(ZM, B)
    multiply(XP, False)
    await_raw(ZP, A)
    normalize(ZP, A)
    multiply(ZM, False)
    multiply(ZP, False)
    multiply(XP, True)
    if meanwhile:
        meanwhile()
    await_raw(Z2, A)
    send_raw(Z2, A, XP, Z2X)
    await_raw(Z2, B)
    send_raw(Z2, B, XP, Z2X)
    normalize(Z2, A)
    normalize(Z2, B)
    multiply(ZM, True)
    multiply(ZP, True)
    multiply(Z2, False)
    multiply(Z2, True)
    await_raw(ZMX, A)
    normalize(ZMX, A)
    await_raw(ZPX, A)
    normalize(ZPX, A)
    await_raw(Z2X, A)
    normalize(Z2X, A)
    await_raw(ZMX, B)
    normalize(ZMX, B)
    await_raw(ZPX, B)
    normalize(ZPX, B)
    multiply(ZMX, False)
    await_raw(Z2X, B)
    normalize(Z2X, B)
    multiply(ZPX, False)
    multiply(Z2X, False)
    multiply(ZMX, True)
    multiply(ZPX, True)
    multiply(Z2X, True)
    for cp in stat_copies + list(sends.values()) + list(d_copies.values()):
        cp.wait_send()


def head_norm_phase(acc, gains, outs, qstat, qsend, qrecv, meanwhile):
    half = acc.shape[1]
    wq = outs[0].shape[1]
    for side in range(2):
        for i in range(2):
            values = acc[side, :, i * wq:(i + 1) * wq]
            qstat[0, 2 * side + i:2 * side + i + 1] = lane_sums(values * values)
    copies = []
    for flip in (False, True):
        for role in range(8):
            if role == OWN and not flip:
                continue
            there = BACK[role] + 8 * flip
            copies.append(
                remote(qstat.at[0], qstat.at[there], qsend.at[role + 8 * flip], qrecv.at[there], hid_device(role, flip))
            )
    for side in range(2):
        outs[2][pl.ds(side * half, half)] = acc[side, :, 2 * wq:3 * wq].astype(BF16)
    meanwhile()
    for cp in copies:
        cp.wait_recv()
    sums = qstat[0]
    for i in range(1, 16):
        sums = sums + qstat[i]
    scales = lax.rsqrt(rows_to_columns(sums * (1.0 / (16 * wq)), 128) + EPS)
    for side in range(2):
        for i in range(2):
            at = (2 * side + i) * 128
            by = scales[:, at:at + 1] * (SCORE_SCALE if i == 0 else 1.0)
            outs[i][pl.ds(side * half, half)] = (acc[side, :, i * wq:(i + 1) * wq] * by * gains[i][...]).astype(BF16)
    for cp in copies:
        cp.wait_send()


def attend_phase(q_ref, k_ref, v_ref, clip_ref, out_ref, qb, kb, vb, crow, best, acc, obuf,
                 xsend, xrecv, ysend, yrecv, csend, crecv, osem):
    rows = q_ref.shape[0]
    tile = rows // 2
    xh = lax.rem(lax.axis_index("seq"), 2)
    mine = pl.ds(pl.multiple_of(xh * HEAD_DIM, HEAD_DIM), HEAD_DIM)
    other = pl.ds(pl.multiple_of((1 - xh) * HEAD_DIM, HEAD_DIM), HEAD_DIM)
    low = pl.ds(0, HEAD_DIM)
    peers = [(y, f) for y in range(4) for f in (0, 1) if (y, f) != (0, 0)]
    def to(src, dst, send_sem, recv_sem, y, f):
        return pltpu.make_async_remote_copy(
            src, dst, send_sem, recv_sem, device_id=seq_device(y, f), device_id_type=MESH
        )

    def clip_copy(y, f):
        there = Y_BACK[y] * 2 + f
        return to(crow.at[0], crow.at[there], csend.at[y * 2 + f], crecv.at[there], y, f)

    x_copies = {
        "k": lambda: to(k_ref.at[:, other], kb.at[1, :, low], xsend.at[0], xrecv.at[0], 0, 1),
        "v": lambda: to(v_ref.at[:, other], vb.at[1, :, low], xsend.at[1], xrecv.at[1], 0, 1),
        "q": lambda: to(q_ref.at[:, other], qb.at[pl.ds(rows, rows), low], xsend.at[2], xrecv.at[2], 0, 1),
    }

    routes = {
        ("k", 2): (0, 2), ("k", 4): (0, 1), ("k", 3): (1, 2), ("k", 5): (1, 1), ("k", 6): (2, 2), ("k", 7): (3, 2),
        ("v", 2): (0, 2), ("v", 4): (0, 1), ("v", 3): (1, 2), ("v", 5): (1, 1), ("v", 6): (4, 1), ("v", 7): (5, 1),
    }

    def y_copy(name, to_slot):
        slot, y_role = routes[name, to_slot]
        buf, which = (kb, 0) if name == "k" else (vb, 1)
        return to(
            buf.at[slot, :, low], buf.at[to_slot, :, low],
            ysend.at[which, to_slot], yrecv.at[which, to_slot], y_role, 0,
        )

    def send_clips():
        crow[0] = clip_ref[...]
        for y, f in peers:
            clip_copy(y, f).start()

    def send_values():
        vb[0, :, 0:HEAD_DIM] = v_ref[:, mine]
        y_copy("v", 4).start()
        y_copy("v", 2).start()
        x_copies["v"]().start()

    def send_keys():
        kb[0, :, 0:HEAD_DIM] = k_ref[:, mine]
        y_copy("k", 2).start()
        y_copy("k", 4).start()
        x_copies["k"]().start()
        x_copies["q"]().start()

    def mark_keys(slot):
        kb[slot, :, HEAD_DIM:2 * HEAD_DIM] = jnp.where(clip_one_hot(crow[slot], HEAD_DIM, HEAD_DIM), 0.0, FAR).astype(BF16)

    def mark_queries(side):
        qb[pl.ds(pl.multiple_of(side * rows, rows), rows), HEAD_DIM:2 * HEAD_DIM] = (
            clip_one_hot(crow[side], HEAD_DIM, HEAD_DIM).astype(F32).astype(BF16)
        )

    def attend_pair(slot, side):
        ats = [pl.ds(pl.multiple_of(side * rows + i * tile, tile), tile) for i in range(2)]
        scores = [
            lax.dot_general(qb[at], kb[slot], (((1,), (1,)), ((), ())), preferred_element_type=F32) for at in ats
        ]
        olds = [best[at] for at in ats]
        before = [acc[at] for at in ats]
        done = []
        for i in range(2):
            old = olds[i][:, 0:1]
            fresh = jnp.maximum(old, jnp.max(scores[i], axis=1, keepdims=True))
            weights = jnp.exp2(scores[i] - fresh).astype(BF16)
            mixed = jnp.dot(weights, vb[slot], preferred_element_type=F32)
            done.append((fresh, before[i] * jnp.exp2(old - fresh) + mixed))
        for i in range(2):
            best[ats[i]] = jnp.broadcast_to(done[i][0], (tile, HEAD_DIM))
            acc[ats[i]] = done[i][1]

    def prepare():
        best[...] = jnp.full(best.shape, 3.0 * FAR, F32)
        acc[...] = jnp.zeros_like(acc)
        for y, f in peers:
            clip_copy(y, f).wait_recv()

        def mark_slot(slot, carry):
            mark_keys(slot)
            vb[slot, :, HEAD_DIM:2 * HEAD_DIM] = jnp.ones((rows, HEAD_DIM), BF16)
            return carry

        def mark_side(side, carry):
            mark_queries(side)
            return carry

        lax.fori_loop(0, 8, mark_slot, 0)
        lax.fori_loop(0, 2, mark_side, 0)

    def early(i, carry):
        @pl.when(i == 1)
        def _():
            y_copy("v", 4).wait_recv()
            y_copy("v", 6).start()
            x_copies["v"]().wait_recv()
            y_copy("v", 5).start()
            y_copy("v", 3).start()
            y_copy("k", 2).wait_recv()
            y_copy("k", 6).start()
            x_copies["k"]().wait_recv()
            y_copy("k", 3).start()
            y_copy("k", 5).start()

        @pl.when(i == 2)
        def _():
            y_copy("v", 2).wait_recv()

        @pl.when(i == 3)
        def _():
            y_copy("k", 4).wait_recv()

        @pl.when(i == 4)
        def _():
            x_copies["q"]().wait_recv()

        j = lax.rem(i, 4)
        attend_pair(j + j // 3, i // 4)
        return carry

    def finished(side):
        at = pl.ds(side * rows, rows)
        return (acc[at, 0:HEAD_DIM] / acc[at, HEAD_DIM:2 * HEAD_DIM]).astype(BF16)

    def back():
        return to(obuf, out_ref.at[:, mine], osem.at[0], osem.at[1], 0, 1)

    def late(i, carry):
        @pl.when(i == 0)
        def _():
            y_copy("k", 3).wait_recv()
            y_copy("k", 7).start()
            y_copy("v", 5).wait_recv()
            y_copy("v", 7).start()
            y_copy("k", 6).wait_recv()
            y_copy("v", 6).wait_recv()

        @pl.when(i == 2)
        def _():
            y_copy("v", 3).wait_recv()

        @pl.when(i == 4)
        def _():
            y_copy("k", 5).wait_recv()

        @pl.when(i == 6)
        def _():
            y_copy("k", 7).wait_recv()
            y_copy("v", 7).wait_recv()

        @pl.when(i == 7)
        def _():
            obuf[...] = finished(1)
            back().start()

        p = i // 2
        attend_pair(6 - 3 * p + 5 * (p // 2) + 5 * (p // 3), lax.rem(i + p // 3, 2))
        return carry

    def run():
        qb[pl.ds(0, rows), 0:HEAD_DIM] = q_ref[:, mine]
        lax.fori_loop(0, 8, early, 0)
        lax.fori_loop(0, 8, late, 0)
        out_ref[:, mine] = finished(0)
        back().wait()
        for y, f in peers:
            clip_copy(y, f).wait_send()
        for name in x_copies:
            x_copies[name]().wait_send()
        for name, slot in routes:
            y_copy(name, slot).wait_send()

    return send_clips, prepare, send_values, send_keys, run


def scatter_phase(a_ref, w_copies, own, hot_ref, gate_ref, wbuf, terms, got, land, gate_buf,
                  dsend, drecv, nsend, nrecv):
    depth, full = wbuf.shape[1], wbuf.shape[2]
    half = got.shape[1]
    part = terms.at[0]
    quarter = half // 2
    core = hid_place()[2]
    d_copies = {}
    arrived = {}

    def multiply(role):
        w_copies[role].wait()

        def row_half(i, carry):
            side = lax.rem(core + i, 2)
            rows = pl.ds(pl.multiple_of(side * half, half), half)
            terms[i, role] = jnp.dot(a_ref[rows], wbuf[role], preferred_element_type=F32).astype(BF16)
            return carry

        lax.fori_loop(0, 2, row_half, 0)
        d_copies[role] = remote(
            terms.at[1, role], got.at[role], dsend.at[role], drecv.at[role], hid_device(OWN, True)
        )

    def send(role, which, to_role, slot):
        rows = pl.ds(which * quarter, quarter)
        arrived[slot, which] = remote(
            part.at[role, rows], land.at[slot, rows], nsend.at[slot, which], nrecv.at[slot, which],
            hid_device(to_role, False),
        )

    def fold(role, which, slots=(), last=False):
        rows = pl.ds(which * quarter, quarter)
        for slot in slots:
            arrived[slot, which].wait_recv()

        def lane_tile(n, carry):
            here = pl.ds(pl.multiple_of(n * 128, 128), 128)
            value = part[role, rows, here].astype(F32) + got[role, rows, here].astype(F32)
            for slot in slots:
                value = value + land[slot, rows, here].astype(F32)
            if last:
                own[rows, here] = (own[rows, here].astype(F32) + gate_buf[rows, here] * value).astype(BF16)
            else:
                part[role, rows, here] = value.astype(BF16)
            return carry

        lax.fori_loop(0, full // 128, lane_tile, 0)

    multiply(Z2X)
    multiply(ZPX)
    multiply(ZMX)
    d_copies[Z2X].wait_recv()
    fold(Z2X, A)
    send(Z2X, A, XP, 0)
    fold(Z2X, B)
    send(Z2X, B, XP, 0)
    d_copies[ZPX].wait_recv()
    fold(ZPX, A)
    send(ZPX, A, ZP, 1)
    d_copies[ZMX].wait_recv()
    fold(ZMX, A)
    send(ZMX, A, ZM, 2)
    fold(ZPX, B)
    send(ZPX, B, ZP, 1)
    fold(ZMX, B)
    send(ZMX, B, ZM, 2)
    multiply(Z2)
    multiply(ZP)
    multiply(ZM)
    d_copies[Z2].wait_recv()
    fold(Z2, A, (0,))
    send(Z2, A, ZP, 3)
    multiply(XP)
    d_copies[ZP].wait_recv()
    fold(ZP, B)
    d_copies[ZM].wait_recv()
    fold(ZM, A)
    d_copies[XP].wait_recv()
    fold(XP, A, (1, 2))
    send(XP, A, XP, 7)
    fold(Z2, B, (0,))
    send(Z2, B, ZM, 4)
    send(ZP, B, ZP, 5)
    send(ZM, A, ZM, 6)
    multiply(OWN)
    fold(XP, B, (1, 2))
    send(XP, B, XP, 7)
    fold(ZP, A, (3,))
    send(ZP, A, ZP, 5)
    fold(ZM, B, (4,))
    send(ZM, B, ZM, 6)
    hot_rows = hot_ref[pl.ds(pl.multiple_of(core * half, half), half)]
    gate_buf[...] = jnp.dot(hot_rows, pieces(gate_ref[...], 3), preferred_element_type=F32)
    d_copies[OWN].wait_recv()
    fold(OWN, A, (7, 6, 5), True)
    fold(OWN, B, (7, 5, 6), True)
    for cp in list(arrived.values()) + list(d_copies.values()):
        cp.wait_send()


def unpair_rows(own, result, theirs, fsem):
    half, full = own.shape
    part = full // 2
    core = hid_place()[2]
    rows = pl.ds(core * half, half)
    values = own[...].astype(F32)
    turned = pltpu.roll(values, part, 1)
    theirs[...] = jnp.where(core == 0, turned, values)[:, 0:part].astype(BF16)
    back = remote(theirs, result.at[rows], fsem.at[0], fsem.at[1], hid_device(OWN, True))
    result[rows] = jnp.where(core == 0, values, turned)[:, 0:part].astype(BF16)
    back.wait()


GATHER_SEMS = [(8,), (8,), (8, 2), (8, 2), (8, 2), (8, 2)]
ATTEND_SEMS = [(3,), (3,), (2, 8), (2, 8), (8,), (8,), (2,)]
SCATTER_SEMS = [(8,), (8,), (8, 2), (8, 2)]


def sems(shapes):
    return [pltpu.SemaphoreType.DMA(s) for s in shapes]


def gather_scratch(half, full, width):
    return [
        pltpu.VMEM((8, half, full), BF16),
        pltpu.VMEM((2, 8, half, full), BF16),
        pltpu.VMEM((8, 2, half), F32),
        pltpu.VMEM((2, half, 128), F32),
        pltpu.VMEM((8, full, width), BF16),
        pltpu.VMEM((2, half, width), F32),
    ]


def attend_scratch(rows):
    return [
        pltpu.VMEM((2 * rows, 2 * HEAD_DIM), BF16),
        pltpu.VMEM((8, rows, 2 * HEAD_DIM), BF16),
        pltpu.VMEM((8, rows, 2 * HEAD_DIM), BF16),
        pltpu.VMEM((8, 1, rows), F32),
        pltpu.VMEM((2 * rows, HEAD_DIM), F32),
        pltpu.VMEM((2 * rows, 2 * HEAD_DIM), F32),
        pltpu.VMEM((rows, HEAD_DIM), BF16),
    ]


def scatter_scratch(half, full):
    return [pltpu.VMEM((8, half, full), BF16), pltpu.VMEM((8, half, full), BF16), pltpu.VMEM((half, full), F32)]


def block_kernel(tokens, clip_ids, clip_step, table, w_query, w_key, w_value, q_gain, k_gain, w_out, w_up, w_down, out_ref,
                 x_turned, clip_ref, mods, gates, x, pair, hot, q, k, v, attended, hidden, qstat, w_first, w_mix,
                 w_last, acc, *refs):
    (x_sem, t_sem, p_sem, w_sem, up_sem, mix_sem, last_sem, qs_sem, qr_sem, free), refs = refs[:10], refs[10:]
    gather_bufs, refs = refs[:4], refs[4:]
    attend_bufs, refs = refs[:7], refs[7:]
    raw = gather_bufs[0]
    scatter_bufs, refs = (gather_bufs[1],) + refs[:3], refs[3:]
    gather_sems, attend_sems, scatter_sems = refs[:6], refs[6:13], refs[13:]
    half = acc.shape[1]
    width = w_query.shape[1]
    wide = w_up.shape[1]

    part, full = x.shape[1], w_last.shape[2]
    x_copy = pltpu.make_async_copy(tokens, x_turned, x_sem.at[0])
    x_copy.start()
    t_copies = [
        pltpu.make_async_copy(table.at[c], mods.at[i], t_sem.at[i]) for i, c in enumerate((0, 1, 3, 4))
    ] + [
        pltpu.make_async_copy(
            table.at[c, :, pl.ds(pl.multiple_of(chip_of(OWN) * full, 128), full)], gates.at[i], t_sem.at[4 + i]
        )
        for i, c in enumerate((2, 5))
    ]
    for cp in t_copies:
        cp.start()
    first = load_columns_of_rows((w_query, w_key, w_value), w_first, w_sem, (width,) * 3)
    clip_ref[...] = clip_ids[...].astype(F32).reshape(clip_ref.shape)
    clip_hot = clip_one_hot(clip_ref[...], 8, 8).astype(F32).astype(BF16)
    steps = lax.dot_general(
        clip_step[...].astype(F32).astype(BF16), jnp.ones((1, hot.shape[1]), BF16), (((0,), (0,)), ((), ())),
        preferred_element_type=F32,
    )
    lane = lax.rem(lax.broadcasted_iota(jnp.int32, steps.shape, 1), hot.shape[1] // 3).astype(F32)
    step_hot = (steps == lane).astype(F32).astype(BF16)
    hot[...] = jnp.dot(clip_hot, step_hot, preferred_element_type=F32).astype(BF16)
    x_copy.wait()
    x[...] = lax.dot_general(
        x_turned[...], identity(part), (((0,), (0,)), ((), ())), preferred_element_type=F32
    ).astype(BF16)
    greet(True, True, True)
    send_clips, prepare, send_values, send_keys, attend = attend_phase(
        q, k, v, clip_ref, attended, *attend_bufs, *attend_sems
    )
    pair_rows(x, raw, pair, p_sem)
    send_clips()
    for cp in t_copies:
        cp.wait()
    gather_phase(hot, mods, 1, first, 3, 3 * width, *gather_bufs, w_first, acc, *gather_sems, meanwhile=prepare)
    head_norm_phase(acc, (q_gain, k_gain), (q, k, v), qstat, qs_sem, qr_sem, send_values)
    send_keys()
    mix = load_blocks_of_columns(w_out, w_mix, mix_sem)
    up = load_columns_of_rows((w_up,), w_first, up_sem, (wide,))
    last = load_blocks_of_columns(w_down, w_last, last_sem)
    attend()
    scatter_phase(attended, mix, raw.at[OWN], hot, gates.at[0], w_mix, *scatter_bufs, *scatter_sems)
    pl.semaphore_signal(free, inc=1, device_id=hid_device(OWN, True), device_id_type=MESH)
    gather_phase(hot, mods, 3, up, 1, wide, *gather_bufs, w_first, acc, *gather_sems, free=free)
    for side in range(2):
        hidden[pl.ds(side * half, half)] = jax.nn.gelu(acc[side, :, 0:wide], approximate=True).astype(BF16)
    scatter_phase(hidden, last, raw.at[OWN], hot, gates.at[1], w_last, *scatter_bufs, *scatter_sems)
    unpair_rows(raw.at[OWN], x, pair, p_sem)
    out_ref[...] = lax.dot_general(
        identity(part), x[...], (((1,), (1,)), ((), ())), preferred_element_type=F32
    ).astype(BF16)


def block(tokens_turned, clip_id, clip_step, table, w_query, w_key, w_value, q_gain, k_gain, w_out, w_up, w_down):
    part, rows = tokens_turned.shape
    steps = table.shape[1]
    half, full = rows // 2, 2 * part
    width, wide = w_query.shape[1], w_up.shape[1]
    gather = gather_scratch(half, full, 3 * width)
    scratch = [
        pltpu.VMEM((part, rows), BF16),
        pltpu.VMEM((1, rows), F32),
        pltpu.VMEM((4, steps, table.shape[2]), F32),
        pltpu.VMEM((2, steps, full), F32),
        pltpu.VMEM((rows, part), BF16),
        pltpu.VMEM((half, part), BF16),
        pltpu.VMEM((rows, 3 * steps), BF16),
        pltpu.VMEM((rows, width), BF16),
        pltpu.VMEM((rows, width), BF16),
        pltpu.VMEM((rows, width), BF16),
        pltpu.VMEM((rows, width), BF16),
        pltpu.VMEM((rows, wide), BF16),
        pltpu.VMEM((16, 4, half), F32),
        gather[4],
        pltpu.VMEM((8, width, full), BF16),
        pltpu.VMEM((8, wide, full), BF16),
        gather[5],
    ]
    scratch += sems([(1,), (6,), (2,), (8, 3), (8, 1), (8,), (8,), (16,), (16,)])
    scratch += [pltpu.SemaphoreType.REGULAR]
    scratch += gather[:4] + attend_scratch(rows) + scatter_scratch(half, full)
    scratch += sems(GATHER_SEMS + ATTEND_SEMS + SCATTER_SEMS)
    return pl.pallas_call(
        block_kernel,
        out_shape=jax.ShapeDtypeStruct((part, rows), BF16),
        in_specs=[ANYSPEC, VSPEC, VSPEC, ANYSPEC, ANYSPEC, ANYSPEC, ANYSPEC, VSPEC, VSPEC, ANYSPEC, ANYSPEC, ANYSPEC],
        out_specs=VSPEC,
        scratch_shapes=scratch,
        compiler_params=pltpu.CompilerParams(collective_id=1, has_side_effects=True, vmem_limit_bytes=60 << 20),
        name="block",
    )(tokens_turned, clip_id, clip_step, table, w_query, w_key, w_value, q_gain, k_gain, w_out, w_up, w_down)


def shards(tokens, clip_id, clip_step, mod_table, w_query, w_key, w_value, q_gain, k_gain, w_out, w_up, w_down):
    return block(
        tokens.T, clip_id, clip_step[None, :], mod_table.transpose(1, 0, 2), w_query, w_key, w_value,
        q_gain[None, :], k_gain[None, :], w_out, w_up, w_down,
    ).T


def solution(mesh):
    placed = (
        P("seq", "hid"), P("seq"), P(), P(), P(None, "hid"), P(None, "hid"), P(None, "hid"), P("hid"), P("hid"),
        P("hid", None), P(None, "hid"), P("hid", None),
    )
    return jax.shard_map(shards, mesh=mesh, in_specs=placed, out_specs=P("seq", "hid"), check_vma=False)
```

```python
import functools
import jax
import jax.numpy as jnp
from jax import lax
from jax.experimental import pallas as pl
from jax.experimental.pallas import tpu as pltpu
from jax.sharding import PartitionSpec as P

MESH = pl.DeviceIdType.MESH
EPS = 1e-06
HEAD_DIM = 128
SCORE_SCALE = HEAD_DIM ** (-0.5) * 1.4426950408889634
FAR = -1e30
F32 = jnp.float32
BF16 = jnp.bfloat16
ANYSPEC = pl.BlockSpec(memory_space=pl.ANY)
VSPEC = pl.BlockSpec(memory_space=pltpu.VMEM)

OWN, XP, ZM, ZP, ZMX, ZPX, Z2, Z2X = range(8)
OFFSETS = ((0, 0), (0, 1), (3, 0), (1, 0), (3, 1), (1, 1), (2, 0), (2, 1))
BACK = (OWN, XP, ZP, ZM, ZPX, ZMX, Z2, Z2X)
Y_STEPS = (0, 3, 1, 2)
Y_BACK = (0, 2, 1, 3)
A, B = 0, 1


def hid_place():
    h = lax.axis_index("hid")
    return h // 4, lax.rem(h // 2, 2), lax.rem(h, 2)


def chip_of(role):
    z, x, _ = hid_place()
    dz, dx = OFFSETS[role]
    return lax.rem(z + dz, 4) * 2 + lax.rem(x + dx, 2)


def hid_device(role, flip):
    core = hid_place()[2]
    core = 1 - core if flip else core
    return {"hid": chip_of(role) * 2 + core}


def seq_device(y_role, flip):
    s = lax.axis_index("seq")
    y, x = s // 2, lax.rem(s, 2)
    x = 1 - x if flip else x
    return {"seq": lax.rem(y + Y_STEPS[y_role], 4) * 2 + x}


def pieces(values, count):
    parts = []
    for i in range(count - 1):
        piece = values.astype(BF16).astype(F32)
        parts.append(piece)
        values = values - piece
    return jnp.concatenate(parts + [values], axis=0).astype(BF16)


def rows_to_columns(rows, width):
    n = rows.shape[0]
    parts = pieces(rows, 3)
    pick = (
        lax.broadcasted_iota(jnp.int32, (3 * n, n * width), 1) // width
        == lax.rem(lax.broadcasted_iota(jnp.int32, (3 * n, n * width), 0), n)
    ).astype(F32).astype(BF16)
    return lax.dot_general(parts, pick, (((0,), (0,)), ((), ())), preferred_element_type=F32)


def identity(size):
    rows = lax.broadcasted_iota(jnp.int32, (size, size), 0)
    return (rows == lax.broadcasted_iota(jnp.int32, (size, size), 1)).astype(F32).astype(BF16)


def lane_sums(values):
    ones = jnp.ones((8, values.shape[1]), BF16)
    dims = (((1,), (1,)), ((), ()))
    if values.dtype == BF16:
        return lax.dot_general(ones, values, dims, preferred_element_type=F32)[0:1]
    top = values.astype(BF16)
    rest = (values - top.astype(F32)).astype(BF16)
    both = lax.dot_general(ones, top, dims, preferred_element_type=F32)
    return (both + lax.dot_general(ones, rest, dims, preferred_element_type=F32))[0:1]


def greet(hid_all, hid_near, seq):
    barrier = pltpu.get_barrier_semaphore()
    peers = [hid_device(OWN, True)]
    if hid_all:
        peers += [hid_device(r, f) for r in range(1, 8) for f in (False, True)]
    elif hid_near:
        peers += [hid_device(r, False) for r in range(1, 8)]
    if seq:
        peers += [seq_device(y, f) for y in range(4) for f in (False, True) if (y, f) != (0, False)]
    for peer in peers:
        pl.semaphore_signal(barrier, inc=1, device_id=peer, device_id_type=MESH)
    return lambda: pl.semaphore_wait(barrier, len(peers))


def remote(src, dst, send_sem, recv_sem, device):
    cp = pltpu.make_async_remote_copy(src, dst, send_sem, recv_sem, device_id=device, device_id_type=MESH)
    cp.start()
    return cp


def clip_one_hot(clip_row, width, period):
    ones = jnp.ones((1, width), BF16)
    cols = lax.dot_general(clip_row.astype(BF16), ones, (((0,), (0,)), ((), ())), preferred_element_type=F32)
    lane = lax.rem(lax.broadcasted_iota(jnp.int32, cols.shape, 1), period).astype(F32)
    return cols == lane


def load_columns_of_rows(w_refs, wbuf, wsem, widths):
    full = wbuf.shape[1]
    copies = {}
    for role in (OWN, ZM, ZP, XP, Z2, ZMX, ZPX, Z2X):
        at = 0
        for i, w_ref in enumerate(w_refs):
            cp = pltpu.make_async_copy(
                w_ref.at[pl.ds(chip_of(role) * full, full)], wbuf.at[role, :, pl.ds(at, widths[i])], wsem.at[role, i]
            )
            cp.start()
            copies[role, i] = cp
            at += widths[i]
    return copies


SCATTER_ORDER = (Z2X, ZPX, ZMX, Z2, ZP, ZM, XP, OWN)


def load_blocks_of_columns(w_ref, wbuf, wsem):
    full = wbuf.shape[2]
    copies = {}
    for role in SCATTER_ORDER:
        cp = pltpu.make_async_copy(
            w_ref.at[:, pl.ds(pl.multiple_of(chip_of(role) * full, 128), full)], wbuf.at[role], wsem.at[role]
        )
        cp.start()
        copies[role] = cp
    return copies


def pair_rows(x_ref, raw, pair, psem):
    half, full = raw.shape[1], raw.shape[2]
    part = full // 2
    core = hid_place()[2]
    swap = remote(
        x_ref.at[pl.ds((1 - core) * half, half)], pair, psem.at[0], psem.at[1], hid_device(OWN, True)
    )

    def place(shift):
        rows = lax.broadcasted_iota(jnp.int32, (part, full), 0)
        cols = lax.broadcasted_iota(jnp.int32, (part, full), 1)
        return (cols == rows + shift).astype(F32).astype(BF16)

    mine = jnp.dot(x_ref[pl.ds(core * half, half)], place(core * part), preferred_element_type=F32)
    swap.wait_recv()
    block = mine + jnp.dot(pair[...], place((1 - core) * part), preferred_element_type=F32)
    raw[OWN] = block.astype(BF16)
    swap.wait_send()


def gather_phase(hot_ref, mod_ref, scale_at, w_copies, n_weights, width,
                 raw, nrm, stat, norm, wbuf, acc, ssend, srecv, rsend, rrecv, dsend, drecv, meanwhile=None, free=None):
    half, full = raw.shape[1], raw.shape[2]
    quarter = half // 2
    core = hid_place()[2]
    sends = {}

    def send_raw(slot, which, to_role, to_slot):
        rows = pl.ds(which * quarter, quarter)
        sends[to_slot, which] = remote(
            raw.at[slot, rows], raw.at[to_slot, rows], rsend.at[to_slot, which], rrecv.at[to_slot, which],
            hid_device(to_role, False),
        )

    def await_raw(slot, which):
        sends[slot, which].wait_recv()

    send_raw(OWN, A, ZP, ZM)
    send_raw(OWN, B, ZM, ZP)
    send_raw(OWN, A, XP, XP)
    block = raw[OWN].astype(F32)
    stat[OWN, 0:1] = lane_sums(raw[OWN])
    stat[OWN, 1:2] = lane_sums(block * block)
    stat_copies = [
        remote(stat.at[OWN], stat.at[BACK[r]], ssend.at[r], srecv.at[BACK[r]], hid_device(r, False))
        for r in range(1, 8)
    ]
    send_raw(OWN, B, ZP, ZM)
    send_raw(OWN, A, ZM, ZP)
    send_raw(OWN, B, XP, XP)
    d_copies = {}
    hot = [hot_ref[pl.ds(pl.multiple_of(core * half + i * quarter, quarter), quarter)] for i in range(2)]
    for cp in stat_copies:
        cp.wait_recv()
    totals = stat[0]
    for r in range(1, 8):
        totals = totals + stat[r]
    moments = rows_to_columns(totals * (1.0 / (full * 8)), 128)
    norm[0] = moments[:, 0:128]
    norm[1] = lax.rsqrt(moments[:, 128:256] - moments[:, 0:128] * moments[:, 0:128] + EPS)

    def normalize(role, which):
        col = chip_of(role) * full
        rows = pl.ds(which * quarter, quarter)

        def lane_tile(n, carry):
            here = pl.ds(pl.multiple_of(n * 128, 128), 128)
            there = pl.ds(pl.multiple_of(col + n * 128, 128), 128)
            scale = jnp.dot(hot[which], pieces(mod_ref[scale_at, :, there], 3), preferred_element_type=F32)
            shift = jnp.dot(hot[which], pieces(mod_ref[scale_at - 1, :, there], 3), preferred_element_type=F32)
            values = (raw[role, rows, here].astype(F32) - norm[0, rows]) * norm[1, rows]
            nrm[core, role, rows, here] = (values * (1.0 + scale) + shift).astype(BF16)
            return carry

        lax.fori_loop(0, full // 128, lane_tile, 0)
        d_copies[role, which] = remote(
            nrm.at[core, role, rows], nrm.at[core, role, rows], dsend.at[role, which], drecv.at[role, which],
            hid_device(OWN, True),
        )

    first = [True, True]

    def multiply(role, theirs):
        side = 1 - core if theirs else core
        if theirs:
            d_copies[role, A].wait_recv()
            d_copies[role, B].wait_recv()
        else:
            for i in range(n_weights):
                w_copies[role, i].wait()
        fresh = first[theirs]
        first[theirs] = False

        def column_tile(n, carry):
            cols = pl.ds(pl.multiple_of(n * 256, 256), 256)
            term = jnp.dot(nrm[side, role], wbuf[role, :, cols], preferred_element_type=F32)
            if fresh:
                acc[side, :, cols] = term
            else:
                acc[side, :, cols] += term
            return carry

        lax.fori_loop(0, width // 256, column_tile, 0)

    if free is not None:
        pl.semaphore_wait(free, 1)
    normalize(OWN, A)
    normalize(OWN, B)
    await_raw(ZM, A)
    send_raw(ZM, A, ZP, Z2)
    await_raw(ZP, B)
    send_raw(ZP, B, ZM, Z2)
    await_raw(XP, A)
    send_raw(XP, A, ZP, ZMX)
    send_raw(XP, A, ZM, ZPX)
    multiply(OWN, False)
    normalize(ZM, A)
    normalize(ZP, B)
    normalize(XP, A)
    multiply(OWN, True)
    if meanwhile:
        meanwhile()
    await_raw(XP, B)
    send_raw(XP, B, ZP, ZMX)
    send_raw(XP, B, ZM, ZPX)
    normalize(XP, B)
    await_raw(ZM, B)
    normalize(ZM, B)
    multiply(XP, False)
    await_raw(ZP, A)
    normalize(ZP, A)
    multiply(ZM, False)
    multiply(ZP, False)
    multiply(XP, True)
    await_raw(Z2, A)
    send_raw(Z2, A, XP, Z2X)
    await_raw(Z2, B)
    send_raw(Z2, B, XP, Z2X)
    normalize(Z2, A)
    normalize(Z2, B)
    multiply(ZM, True)
    multiply(ZP, True)
    multiply(Z2, False)
    multiply(Z2, True)
    await_raw(ZMX, A)
    normalize(ZMX, A)
    await_raw(ZPX, A)
    normalize(ZPX, A)
    await_raw(Z2X, A)
    normalize(Z2X, A)
    await_raw(ZMX, B)
    normalize(ZMX, B)
    await_raw(ZPX, B)
    normalize(ZPX, B)
    multiply(ZMX, False)
    await_raw(Z2X, B)
    normalize(Z2X, B)
    multiply(ZPX, False)
    multiply(Z2X, False)
    multiply(ZMX, True)
    multiply(ZPX, True)
    multiply(Z2X, True)
    for cp in stat_copies + list(sends.values()) + list(d_copies.values()):
        cp.wait_send()


def head_norm_phase(acc, gains, outs, qstat, qsend, qrecv, meanwhile):
    half = acc.shape[1]
    wq = outs[0].shape[1]
    for side in range(2):
        for i in range(2):
            values = acc[side, :, i * wq:(i + 1) * wq]
            qstat[0, 2 * side + i:2 * side + i + 1] = lane_sums(values * values)
    copies = []
    for flip in (False, True):
        for role in range(8):
            if role == OWN and not flip:
                continue
            there = BACK[role] + 8 * flip
            copies.append(
                remote(qstat.at[0], qstat.at[there], qsend.at[role + 8 * flip], qrecv.at[there], hid_device(role, flip))
            )
    for side in range(2):
        outs[2][pl.ds(side * half, half)] = acc[side, :, 2 * wq:3 * wq].astype(BF16)
    meanwhile()
    for cp in copies:
        cp.wait_recv()
    sums = qstat[0]
    for i in range(1, 16):
        sums = sums + qstat[i]
    scales = lax.rsqrt(rows_to_columns(sums * (1.0 / (16 * wq)), 128) + EPS)
    for side in range(2):
        for i in range(2):
            at = (2 * side + i) * 128
            by = scales[:, at:at + 1] * (SCORE_SCALE if i == 0 else 1.0)
            outs[i][pl.ds(side * half, half)] = (acc[side, :, i * wq:(i + 1) * wq] * by * gains[i][...]).astype(BF16)
    for cp in copies:
        cp.wait_send()


def attend_phase(q_ref, k_ref, v_ref, clip_ref, out_ref, qb, kb, vb, crow, best, acc, obuf,
                 xsend, xrecv, ysend, yrecv, csend, crecv, osem):
    rows = q_ref.shape[0]
    tile = rows // 2
    xh = lax.rem(lax.axis_index("seq"), 2)
    mine = pl.ds(pl.multiple_of(xh * HEAD_DIM, HEAD_DIM), HEAD_DIM)
    other = pl.ds(pl.multiple_of((1 - xh) * HEAD_DIM, HEAD_DIM), HEAD_DIM)
    low = pl.ds(0, HEAD_DIM)
    peers = [(y, f) for y in range(4) for f in (0, 1) if (y, f) != (0, 0)]
    def to(src, dst, send_sem, recv_sem, y, f):
        return pltpu.make_async_remote_copy(
            src, dst, send_sem, recv_sem, device_id=seq_device(y, f), device_id_type=MESH
        )

    def clip_copy(y, f):
        there = Y_BACK[y] * 2 + f
        return to(crow.at[0], crow.at[there], csend.at[y * 2 + f], crecv.at[there], y, f)

    x_copies = {
        "k": lambda: to(k_ref.at[:, other], kb.at[1, :, low], xsend.at[0], xrecv.at[0], 0, 1),
        "v": lambda: to(v_ref.at[:, other], vb.at[1, :, low], xsend.at[1], xrecv.at[1], 0, 1),
        "q": lambda: to(q_ref.at[:, other], qb.at[pl.ds(rows, rows), low], xsend.at[2], xrecv.at[2], 0, 1),
    }

    routes = {
        ("k", 2): (0, 2), ("k", 4): (0, 1), ("k", 3): (1, 2), ("k", 5): (1, 1), ("k", 6): (2, 2), ("k", 7): (3, 2),
        ("v", 2): (0, 2), ("v", 4): (0, 1), ("v", 3): (1, 2), ("v", 5): (1, 1), ("v", 6): (4, 1), ("v", 7): (5, 1),
    }

    def y_copy(name, to_slot):
        slot, y_role = routes[name, to_slot]
        buf, which = (kb, 0) if name == "k" else (vb, 1)
        return to(
            buf.at[slot, :, low], buf.at[to_slot, :, low],
            ysend.at[which, to_slot], yrecv.at[which, to_slot], y_role, 0,
        )

    def send_clips():
        crow[0] = clip_ref[...]
        for y, f in peers:
            clip_copy(y, f).start()

    def send_values():
        vb[0, :, 0:HEAD_DIM] = v_ref[:, mine]
        y_copy("v", 4).start()
        y_copy("v", 2).start()
        x_copies["v"]().start()

    def send_keys():
        kb[0, :, 0:HEAD_DIM] = k_ref[:, mine]
        y_copy("k", 2).start()
        y_copy("k", 4).start()
        x_copies["k"]().start()

    def mark_keys(slot):
        kb[slot, :, HEAD_DIM:2 * HEAD_DIM] = jnp.where(clip_one_hot(crow[slot], HEAD_DIM, HEAD_DIM), 0.0, FAR).astype(BF16)

    def mark_queries(side):
        qb[pl.ds(pl.multiple_of(side * rows, rows), rows), HEAD_DIM:2 * HEAD_DIM] = (
            clip_one_hot(crow[side], HEAD_DIM, HEAD_DIM).astype(F32).astype(BF16)
        )

    def attend_pair(slot, side):
        ats = [pl.ds(pl.multiple_of(side * rows + i * tile, tile), tile) for i in range(2)]
        scores = [
            lax.dot_general(qb[at], kb[slot], (((1,), (1,)), ((), ())), preferred_element_type=F32) for at in ats
        ]
        olds = [best[at] for at in ats]
        before = [acc[at] for at in ats]
        done = []
        for i in range(2):
            old = olds[i][:, 0:1]
            fresh = jnp.maximum(old, jnp.max(scores[i], axis=1, keepdims=True))
            weights = jnp.exp2(scores[i] - fresh).astype(BF16)
            mixed = jnp.dot(weights, vb[slot], preferred_element_type=F32)
            done.append((fresh, before[i] * jnp.exp2(old - fresh) + mixed))
        for i in range(2):
            best[ats[i]] = jnp.broadcast_to(done[i][0], (tile, HEAD_DIM))
            acc[ats[i]] = done[i][1]

    def prepare():
        best[...] = jnp.full(best.shape, 3.0 * FAR, F32)
        acc[...] = jnp.zeros_like(acc)
        for y, f in peers:
            clip_copy(y, f).wait_recv()

        def mark_slot(slot, carry):
            mark_keys(slot)
            vb[slot, :, HEAD_DIM:2 * HEAD_DIM] = jnp.ones((rows, HEAD_DIM), BF16)
            return carry

        def mark_side(side, carry):
            mark_queries(side)
            return carry

        lax.fori_loop(0, 8, mark_slot, 0)
        lax.fori_loop(0, 2, mark_side, 0)

    def early(i, carry):
        @pl.when(i == 1)
        def _():
            x_copies["v"]().wait_recv()
            y_copy("v", 5).start()
            x_copies["k"]().wait_recv()
            y_copy("k", 3).start()
            x_copies["q"]().start()
            y_copy("k", 2).wait_recv()
            y_copy("v", 4).wait_recv()
            y_copy("k", 6).start()
            y_copy("v", 6).start()
            y_copy("v", 3).start()
            y_copy("k", 5).start()

        @pl.when(i == 2)
        def _():
            y_copy("v", 2).wait_recv()

        @pl.when(i == 3)
        def _():
            y_copy("k", 4).wait_recv()

        @pl.when(i == 4)
        def _():
            x_copies["q"]().wait_recv()

        j = lax.rem(i, 4)
        attend_pair(j + j // 3, i // 4)
        return carry

    def finished(side):
        at = pl.ds(side * rows, rows)
        return (acc[at, 0:HEAD_DIM] / acc[at, HEAD_DIM:2 * HEAD_DIM]).astype(BF16)

    def back():
        return to(obuf, out_ref.at[:, mine], osem.at[0], osem.at[1], 0, 1)

    def late(i, carry):
        @pl.when(i == 0)
        def _():
            y_copy("k", 3).wait_recv()
            y_copy("k", 7).start()
            y_copy("v", 5).wait_recv()
            y_copy("v", 7).start()
            y_copy("k", 6).wait_recv()
            y_copy("v", 6).wait_recv()

        @pl.when(i == 2)
        def _():
            y_copy("v", 3).wait_recv()

        @pl.when(i == 4)
        def _():
            y_copy("k", 5).wait_recv()

        @pl.when(i == 6)
        def _():
            y_copy("k", 7).wait_recv()
            y_copy("v", 7).wait_recv()

        @pl.when(i == 7)
        def _():
            obuf[...] = finished(1)
            back().start()

        p = i // 2
        attend_pair(6 - 3 * p + 5 * (p // 2) + 5 * (p // 3), lax.rem(i + p // 3, 2))
        return carry

    def run():
        qb[pl.ds(0, rows), 0:HEAD_DIM] = q_ref[:, mine]
        lax.fori_loop(0, 8, early, 0)
        lax.fori_loop(0, 8, late, 0)
        out_ref[:, mine] = finished(0)
        back().wait()
        for y, f in peers:
            clip_copy(y, f).wait_send()
        for name in x_copies:
            x_copies[name]().wait_send()
        for name, slot in routes:
            y_copy(name, slot).wait_send()

    return send_clips, prepare, send_values, send_keys, run


def scatter_phase(a_ref, w_copies, own, hot_ref, gate_ref, wbuf, terms, got, land, gate_buf,
                  dsend, drecv, nsend, nrecv):
    depth, full = wbuf.shape[1], wbuf.shape[2]
    half = got.shape[1]
    part = terms.at[0]
    quarter = half // 2
    core = hid_place()[2]
    d_copies = {}
    arrived = {}

    def multiply(role):
        w_copies[role].wait()

        def row_half(i, carry):
            side = lax.rem(core + i, 2)
            rows = pl.ds(pl.multiple_of(side * half, half), half)
            terms[i, role] = jnp.dot(a_ref[rows], wbuf[role], preferred_element_type=F32).astype(BF16)
            return carry

        lax.fori_loop(0, 2, row_half, 0)
        d_copies[role] = remote(
            terms.at[1, role], got.at[role], dsend.at[role], drecv.at[role], hid_device(OWN, True)
        )

    def send(role, which, to_role, slot):
        rows = pl.ds(which * quarter, quarter)
        arrived[slot, which] = remote(
            part.at[role, rows], land.at[slot, rows], nsend.at[slot, which], nrecv.at[slot, which],
            hid_device(to_role, False),
        )

    def fold(role, which, slots=(), last=False):
        rows = pl.ds(which * quarter, quarter)
        for slot in slots:
            arrived[slot, which].wait_recv()

        def lane_tile(n, carry):
            here = pl.ds(pl.multiple_of(n * 128, 128), 128)
            value = part[role, rows, here].astype(F32) + got[role, rows, here].astype(F32)
            for slot in slots:
                value = value + land[slot, rows, here].astype(F32)
            if last:
                own[rows, here] = (own[rows, here].astype(F32) + gate_buf[rows, here] * value).astype(BF16)
            else:
                part[role, rows, here] = value.astype(BF16)
            return carry

        lax.fori_loop(0, full // 128, lane_tile, 0)

    multiply(Z2X)
    multiply(ZPX)
    multiply(ZMX)
    d_copies[Z2X].wait_recv()
    fold(Z2X, A)
    send(Z2X, A, XP, 0)
    fold(Z2X, B)
    send(Z2X, B, XP, 0)
    d_copies[ZPX].wait_recv()
    fold(ZPX, A)
    send(ZPX, A, ZP, 1)
    d_copies[ZMX].wait_recv()
    fold(ZMX, A)
    send(ZMX, A, ZM, 2)
    fold(ZPX, B)
    send(ZPX, B, ZP, 1)
    fold(ZMX, B)
    send(ZMX, B, ZM, 2)
    multiply(Z2)
    multiply(ZP)
    multiply(ZM)
    d_copies[Z2].wait_recv()
    fold(Z2, A, (0,))
    send(Z2, A, ZP, 3)
    multiply(XP)
    d_copies[ZP].wait_recv()
    fold(ZP, B)
    d_copies[ZM].wait_recv()
    fold(ZM, A)
    d_copies[XP].wait_recv()
    fold(XP, A, (1, 2))
    send(XP, A, XP, 7)
    fold(Z2, B, (0,))
    send(Z2, B, ZM, 4)
    send(ZP, B, ZP, 5)
    send(ZM, A, ZM, 6)
    multiply(OWN)
    fold(XP, B, (1, 2))
    send(XP, B, XP, 7)
    fold(ZP, A, (3,))
    send(ZP, A, ZP, 5)
    fold(ZM, B, (4,))
    send(ZM, B, ZM, 6)
    hot_rows = hot_ref[pl.ds(pl.multiple_of(core * half, half), half)]
    gate_buf[...] = jnp.dot(hot_rows, pieces(gate_ref[...], 3), preferred_element_type=F32)
    d_copies[OWN].wait_recv()
    fold(OWN, A, (7, 6, 5), True)
    fold(OWN, B, (7, 5, 6), True)
    for cp in list(arrived.values()) + list(d_copies.values()):
        cp.wait_send()


def unpair_rows(own, result, theirs, fsem):
    half, full = own.shape
    part = full // 2
    core = hid_place()[2]
    rows = pl.ds(core * half, half)
    values = own[...].astype(F32)
    turned = pltpu.roll(values, part, 1)
    theirs[...] = jnp.where(core == 0, turned, values)[:, 0:part].astype(BF16)
    back = remote(theirs, result.at[rows], fsem.at[0], fsem.at[1], hid_device(OWN, True))
    result[rows] = jnp.where(core == 0, values, turned)[:, 0:part].astype(BF16)
    back.wait()


GATHER_SEMS = [(8,), (8,), (8, 2), (8, 2), (8, 2), (8, 2)]
ATTEND_SEMS = [(3,), (3,), (2, 8), (2, 8), (8,), (8,), (2,)]
SCATTER_SEMS = [(8,), (8,), (8, 2), (8, 2)]


def sems(shapes):
    return [pltpu.SemaphoreType.DMA(s) for s in shapes]


def gather_scratch(half, full, width):
    return [
        pltpu.VMEM((8, half, full), BF16),
        pltpu.VMEM((2, 8, half, full), BF16),
        pltpu.VMEM((8, 2, half), F32),
        pltpu.VMEM((2, half, 128), F32),
        pltpu.VMEM((8, full, width), BF16),
        pltpu.VMEM((2, half, width), F32),
    ]


def attend_scratch(rows):
    return [
        pltpu.VMEM((2 * rows, 2 * HEAD_DIM), BF16),
        pltpu.VMEM((8, rows, 2 * HEAD_DIM), BF16),
        pltpu.VMEM((8, rows, 2 * HEAD_DIM), BF16),
        pltpu.VMEM((8, 1, rows), F32),
        pltpu.VMEM((2 * rows, HEAD_DIM), F32),
        pltpu.VMEM((2 * rows, 2 * HEAD_DIM), F32),
        pltpu.VMEM((rows, HEAD_DIM), BF16),
    ]


def scatter_scratch(half, full):
    return [pltpu.VMEM((8, half, full), BF16), pltpu.VMEM((8, half, full), BF16), pltpu.VMEM((half, full), F32)]


def block_kernel(tokens, clip_ids, clip_step, table, w_query, w_key, w_value, q_gain, k_gain, w_out, w_up, w_down, out_ref,
                 x_turned, clip_ref, mods, gates, x, pair, hot, q, k, v, attended, hidden, qstat, w_first, w_mix,
                 w_last, acc, *refs):
    (x_sem, t_sem, p_sem, w_sem, up_sem, mix_sem, last_sem, qs_sem, qr_sem, free), refs = refs[:10], refs[10:]
    gather_bufs, refs = refs[:4], refs[4:]
    attend_bufs, refs = refs[:7], refs[7:]
    raw = gather_bufs[0]
    scatter_bufs, refs = (gather_bufs[1],) + refs[:3], refs[3:]
    gather_sems, attend_sems, scatter_sems = refs[:6], refs[6:13], refs[13:]
    half = acc.shape[1]
    width = w_query.shape[1]
    wide = w_up.shape[1]

    part, full = x.shape[1], w_last.shape[2]
    x_copy = pltpu.make_async_copy(tokens, x_turned, x_sem.at[0])
    x_copy.start()
    everyone_here = greet(True, True, True)
    t_copies = [
        pltpu.make_async_copy(table.at[c], mods.at[i], t_sem.at[i]) for i, c in enumerate((0, 1, 3, 4))
    ] + [
        pltpu.make_async_copy(
            table.at[c, :, pl.ds(pl.multiple_of(chip_of(OWN) * full, 128), full)], gates.at[i], t_sem.at[4 + i]
        )
        for i, c in enumerate((2, 5))
    ]
    for cp in t_copies:
        cp.start()
    first = load_columns_of_rows((w_query, w_key, w_value), w_first, w_sem, (width,) * 3)
    clip_ref[...] = clip_ids[...].astype(F32).reshape(clip_ref.shape)
    clip_hot = clip_one_hot(clip_ref[...], 8, 8).astype(F32).astype(BF16)
    steps = lax.dot_general(
        clip_step[...].astype(F32).astype(BF16), jnp.ones((1, hot.shape[1]), BF16), (((0,), (0,)), ((), ())),
        preferred_element_type=F32,
    )
    lane = lax.rem(lax.broadcasted_iota(jnp.int32, steps.shape, 1), hot.shape[1] // 3).astype(F32)
    step_hot = (steps == lane).astype(F32).astype(BF16)
    hot[...] = jnp.dot(clip_hot, step_hot, preferred_element_type=F32).astype(BF16)
    x_copy.wait()
    x[...] = lax.dot_general(
        x_turned[...], identity(part), (((0,), (0,)), ((), ())), preferred_element_type=F32
    ).astype(BF16)
    everyone_here()
    send_clips, prepare, send_values, send_keys, attend = attend_phase(
        q, k, v, clip_ref, attended, *attend_bufs, *attend_sems
    )
    pair_rows(x, raw, pair, p_sem)
    send_clips()
    for cp in t_copies:
        cp.wait()
    mix = load_blocks_of_columns(w_out, w_mix, mix_sem)
    last = load_blocks_of_columns(w_down, w_last, last_sem)
    gather_phase(hot, mods, 1, first, 3, 3 * width, *gather_bufs, w_first, acc, *gather_sems, meanwhile=prepare)
    head_norm_phase(acc, (q_gain, k_gain), (q, k, v), qstat, qs_sem, qr_sem, send_values)
    send_keys()
    attend()
    up = load_columns_of_rows((w_up,), w_first, up_sem, (wide,))
    scatter_phase(attended, mix, raw.at[OWN], hot, gates.at[0], w_mix, *scatter_bufs, *scatter_sems)
    pl.semaphore_signal(free, inc=1, device_id=hid_device(OWN, True), device_id_type=MESH)
    gather_phase(hot, mods, 3, up, 1, wide, *gather_bufs, w_first, acc, *gather_sems, free=free)
    for side in range(2):
        hidden[pl.ds(side * half, half)] = jax.nn.gelu(acc[side, :, 0:wide], approximate=True).astype(BF16)
    scatter_phase(hidden, last, raw.at[OWN], hot, gates.at[1], w_last, *scatter_bufs, *scatter_sems)
    unpair_rows(raw.at[OWN], x, pair, p_sem)
    out_ref[...] = lax.dot_general(
        identity(part), x[...], (((1,), (1,)), ((), ())), preferred_element_type=F32
    ).astype(BF16)


def block(tokens_turned, clip_id, clip_step, table, w_query, w_key, w_value, q_gain, k_gain, w_out, w_up, w_down):
    part, rows = tokens_turned.shape
    steps = table.shape[1]
    half, full = rows // 2, 2 * part
    width, wide = w_query.shape[1], w_up.shape[1]
    gather = gather_scratch(half, full, 3 * width)
    scratch = [
        pltpu.VMEM((part, rows), BF16),
        pltpu.VMEM((1, rows), F32),
        pltpu.VMEM((4, steps, table.shape[2]), F32),
        pltpu.VMEM((2, steps, full), F32),
        pltpu.VMEM((rows, part), BF16),
        pltpu.VMEM((half, part), BF16),
        pltpu.VMEM((rows, 3 * steps), BF16),
        pltpu.VMEM((rows, width), BF16),
        pltpu.VMEM((rows, width), BF16),
        pltpu.VMEM((rows, width), BF16),
        pltpu.VMEM((rows, width), BF16),
        pltpu.VMEM((rows, wide), BF16),
        pltpu.VMEM((16, 4, half), F32),
        gather[4],
        pltpu.VMEM((8, width, full), BF16),
        pltpu.VMEM((8, wide, full), BF16),
        gather[5],
    ]
    scratch += sems([(1,), (6,), (2,), (8, 3), (8, 1), (8,), (8,), (16,), (16,)])
    scratch += [pltpu.SemaphoreType.REGULAR]
    scratch += gather[:4] + attend_scratch(rows) + scatter_scratch(half, full)
    scratch += sems(GATHER_SEMS + ATTEND_SEMS + SCATTER_SEMS)
    return pl.pallas_call(
        block_kernel,
        out_shape=jax.ShapeDtypeStruct((part, rows), BF16),
        in_specs=[ANYSPEC, VSPEC, VSPEC, ANYSPEC, ANYSPEC, ANYSPEC, ANYSPEC, VSPEC, VSPEC, ANYSPEC, ANYSPEC, ANYSPEC],
        out_specs=VSPEC,
        scratch_shapes=scratch,
        compiler_params=pltpu.CompilerParams(collective_id=1, has_side_effects=True, vmem_limit_bytes=60 << 20),
        name="block",
    )(tokens_turned, clip_id, clip_step, table, w_query, w_key, w_value, q_gain, k_gain, w_out, w_up, w_down)


def shards(tokens, clip_id, clip_step, mod_table, w_query, w_key, w_value, q_gain, k_gain, w_out, w_up, w_down):
    return block(
        tokens.T, clip_id, clip_step[None, :], mod_table.transpose(1, 0, 2), w_query, w_key, w_value,
        q_gain[None, :], k_gain[None, :], w_out, w_up, w_down,
    ).T


def solution(mesh):
    placed = (
        P("seq", "hid"), P("seq"), P(), P(), P(None, "hid"), P(None, "hid"), P(None, "hid"), P("hid"), P("hid"),
        P("hid", None), P(None, "hid"), P("hid", None),
    )
    return jax.shard_map(shards, mesh=mesh, in_specs=placed, out_specs=P("seq", "hid"), check_vma=False)
```

```python
import functools
import jax
import jax.numpy as jnp
from jax import lax
from jax.experimental import pallas as pl
from jax.experimental.pallas import tpu as pltpu
from jax.sharding import PartitionSpec as P

MESH = pl.DeviceIdType.MESH
EPS = 1e-06
HEAD_DIM = 128
SCORE_SCALE = HEAD_DIM ** (-0.5) * 1.4426950408889634
FAR = -1e30
F32 = jnp.float32
BF16 = jnp.bfloat16
ANYSPEC = pl.BlockSpec(memory_space=pl.ANY)
VSPEC = pl.BlockSpec(memory_space=pltpu.VMEM)

OWN, XP, ZM, ZP, ZMX, ZPX, Z2, Z2X = range(8)
OFFSETS = ((0, 0), (0, 1), (3, 0), (1, 0), (3, 1), (1, 1), (2, 0), (2, 1))
BACK = (OWN, XP, ZP, ZM, ZPX, ZMX, Z2, Z2X)
Y_STEPS = (0, 3, 1, 2)
Y_BACK = (0, 2, 1, 3)
A, B = 0, 1


def hid_place():
    h = lax.axis_index("hid")
    return h // 4, lax.rem(h // 2, 2), lax.rem(h, 2)


def chip_of(role):
    z, x, _ = hid_place()
    dz, dx = OFFSETS[role]
    return lax.rem(z + dz, 4) * 2 + lax.rem(x + dx, 2)


def hid_device(role, flip):
    core = hid_place()[2]
    core = 1 - core if flip else core
    return {"hid": chip_of(role) * 2 + core}


def seq_device(y_role, flip):
    s = lax.axis_index("seq")
    y, x = s // 2, lax.rem(s, 2)
    x = 1 - x if flip else x
    return {"seq": lax.rem(y + Y_STEPS[y_role], 4) * 2 + x}


def pieces(values, count):
    parts = []
    for i in range(count - 1):
        piece = values.astype(BF16).astype(F32)
        parts.append(piece)
        values = values - piece
    return jnp.concatenate(parts + [values], axis=0).astype(BF16)


def rows_to_columns(rows, width):
    n = rows.shape[0]
    parts = pieces(rows, 3)
    pick = (
        lax.broadcasted_iota(jnp.int32, (3 * n, n * width), 1) // width
        == lax.rem(lax.broadcasted_iota(jnp.int32, (3 * n, n * width), 0), n)
    ).astype(F32).astype(BF16)
    return lax.dot_general(parts, pick, (((0,), (0,)), ((), ())), preferred_element_type=F32)


def identity(size):
    rows = lax.broadcasted_iota(jnp.int32, (size, size), 0)
    return (rows == lax.broadcasted_iota(jnp.int32, (size, size), 1)).astype(F32).astype(BF16)


def lane_sums(values):
    ones = jnp.ones((8, values.shape[1]), BF16)
    dims = (((1,), (1,)), ((), ()))
    if values.dtype == BF16:
        return lax.dot_general(ones, values, dims, preferred_element_type=F32)[0:1]
    top = values.astype(BF16)
    rest = (values - top.astype(F32)).astype(BF16)
    both = lax.dot_general(ones, top, dims, preferred_element_type=F32)
    return (both + lax.dot_general(ones, rest, dims, preferred_element_type=F32))[0:1]


def greet(hid_all, hid_near, seq):
    barrier = pltpu.get_barrier_semaphore()
    peers = [hid_device(OWN, True)]
    if hid_all:
        peers += [hid_device(r, f) for r in range(1, 8) for f in (False, True)]
    elif hid_near:
        peers += [hid_device(r, False) for r in range(1, 8)]
    if seq:
        peers += [seq_device(y, f) for y in range(4) for f in (False, True) if (y, f) != (0, False)]
    for peer in peers:
        pl.semaphore_signal(barrier, inc=1, device_id=peer, device_id_type=MESH)
    return lambda: pl.semaphore_wait(barrier, len(peers))


def remote(src, dst, send_sem, recv_sem, device):
    cp = pltpu.make_async_remote_copy(src, dst, send_sem, recv_sem, device_id=device, device_id_type=MESH)
    cp.start()
    return cp


def clip_one_hot(clip_row, width, period):
    ones = jnp.ones((1, width), BF16)
    cols = lax.dot_general(clip_row.astype(BF16), ones, (((0,), (0,)), ((), ())), preferred_element_type=F32)
    lane = lax.rem(lax.broadcasted_iota(jnp.int32, cols.shape, 1), period).astype(F32)
    return cols == lane


def load_columns_of_rows(w_refs, wbuf, wsem, widths):
    full = wbuf.shape[1]
    copies = {}
    for role in (OWN, ZM, ZP, XP, Z2, ZMX, ZPX, Z2X):
        at = 0
        for i, w_ref in enumerate(w_refs):
            cp = pltpu.make_async_copy(
                w_ref.at[pl.ds(chip_of(role) * full, full)], wbuf.at[role, :, pl.ds(at, widths[i])], wsem.at[role, i]
            )
            cp.start()
            copies[role, i] = cp
            at += widths[i]
    return copies


SCATTER_ORDER = (Z2X, ZPX, ZMX, Z2, ZP, ZM, XP, OWN)


def load_blocks_of_columns(w_ref, wbuf, wsem):
    full = wbuf.shape[2]
    copies = {}
    for role in SCATTER_ORDER:
        cp = pltpu.make_async_copy(
            w_ref.at[:, pl.ds(pl.multiple_of(chip_of(role) * full, 128), full)], wbuf.at[role], wsem.at[role]
        )
        cp.start()
        copies[role] = cp
    return copies


def pair_rows(x_ref, raw, pair, psem):
    half, full = raw.shape[1], raw.shape[2]
    part = full // 2
    core = hid_place()[2]
    swap = remote(
        x_ref.at[pl.ds((1 - core) * half, half)], pair, psem.at[0], psem.at[1], hid_device(OWN, True)
    )

    def place(shift):
        rows = lax.broadcasted_iota(jnp.int32, (part, full), 0)
        cols = lax.broadcasted_iota(jnp.int32, (part, full), 1)
        return (cols == rows + shift).astype(F32).astype(BF16)

    mine = jnp.dot(x_ref[pl.ds(core * half, half)], place(core * part), preferred_element_type=F32)
    swap.wait_recv()
    block = mine + jnp.dot(pair[...], place((1 - core) * part), preferred_element_type=F32)
    raw[OWN] = block.astype(BF16)
    swap.wait_send()


def gather_phase(hot_ref, mod_ref, scale_at, w_copies, n_weights, width,
                 raw, nrm, stat, norm, wbuf, acc, ssend, srecv, rsend, rrecv, dsend, drecv, meanwhile=None, free=None):
    half, full = raw.shape[1], raw.shape[2]
    quarter = half // 2
    core = hid_place()[2]
    sends = {}

    def send_raw(slot, which, to_role, to_slot):
        rows = pl.ds(which * quarter, quarter)
        sends[to_slot, which] = remote(
            raw.at[slot, rows], raw.at[to_slot, rows], rsend.at[to_slot, which], rrecv.at[to_slot, which],
            hid_device(to_role, False),
        )

    def await_raw(slot, which):
        sends[slot, which].wait_recv()

    send_raw(OWN, A, ZP, ZM)
    send_raw(OWN, B, ZM, ZP)
    send_raw(OWN, A, XP, XP)
    block = raw[OWN].astype(F32)
    stat[OWN, 0:1] = lane_sums(raw[OWN])
    stat[OWN, 1:2] = lane_sums(block * block)
    stat_copies = [
        remote(stat.at[OWN], stat.at[BACK[r]], ssend.at[r], srecv.at[BACK[r]], hid_device(r, False))
        for r in range(1, 8)
    ]
    send_raw(OWN, B, ZP, ZM)
    send_raw(OWN, A, ZM, ZP)
    send_raw(OWN, B, XP, XP)
    d_copies = {}
    hot = [hot_ref[pl.ds(pl.multiple_of(core * half + i * quarter, quarter), quarter)] for i in range(2)]
    for cp in stat_copies:
        cp.wait_recv()
    totals = stat[0]
    for r in range(1, 8):
        totals = totals + stat[r]
    moments = rows_to_columns(totals * (1.0 / (full * 8)), 128)
    norm[0] = moments[:, 0:128]
    norm[1] = lax.rsqrt(moments[:, 128:256] - moments[:, 0:128] * moments[:, 0:128] + EPS)

    def normalize(role, which):
        col = chip_of(role) * full
        rows = pl.ds(which * quarter, quarter)

        def lane_tile(n, carry):
            here = pl.ds(pl.multiple_of(n * 128, 128), 128)
            there = pl.ds(pl.multiple_of(col + n * 128, 128), 128)
            scale = jnp.dot(hot[which], pieces(mod_ref[scale_at, :, there], 3), preferred_element_type=F32)
            shift = jnp.dot(hot[which], pieces(mod_ref[scale_at - 1, :, there], 3), preferred_element_type=F32)
            values = (raw[role, rows, here].astype(F32) - norm[0, rows]) * norm[1, rows]
            nrm[core, role, rows, here] = (values * (1.0 + scale) + shift).astype(BF16)
            return carry

        lax.fori_loop(0, full // 128, lane_tile, 0)
        d_copies[role, which] = remote(
            nrm.at[core, role, rows], nrm.at[core, role, rows], dsend.at[role, which], drecv.at[role, which],
            hid_device(OWN, True),
        )

    first = [True, True]

    def multiply(role, theirs):
        side = 1 - core if theirs else core
        if theirs:
            d_copies[role, A].wait_recv()
            d_copies[role, B].wait_recv()
        else:
            for i in range(n_weights):
                w_copies[role, i].wait()
        fresh = first[theirs]
        first[theirs] = False

        def column_tile(n, carry):
            cols = pl.ds(pl.multiple_of(n * 256, 256), 256)
            term = jnp.dot(nrm[side, role], wbuf[role, :, cols], preferred_element_type=F32)
            if fresh:
                acc[side, :, cols] = term
            else:
                acc[side, :, cols] += term
            return carry

        lax.fori_loop(0, width // 256, column_tile, 0)

    if free is not None:
        pl.semaphore_wait(free, 1)
    normalize(OWN, A)
    normalize(OWN, B)
    await_raw(ZM, A)
    send_raw(ZM, A, ZP, Z2)
    await_raw(ZP, B)
    send_raw(ZP, B, ZM, Z2)
    await_raw(XP, A)
    send_raw(XP, A, ZP, ZMX)
    send_raw(XP, A, ZM, ZPX)
    multiply(OWN, False)
    normalize(ZM, A)
    normalize(ZP, B)
    normalize(XP, A)
    multiply(OWN, True)
    if meanwhile:
        meanwhile()
    await_raw(XP, B)
    send_raw(XP, B, ZP, ZMX)
    send_raw(XP, B, ZM, ZPX)
    normalize(XP, B)
    await_raw(ZM, B)
    normalize(ZM, B)
    multiply(XP, False)
    await_raw(ZP, A)
    normalize(ZP, A)
    multiply(ZM, False)
    multiply(ZP, False)
    multiply(XP, True)
    await_raw(Z2, A)
    send_raw(Z2, A, XP, Z2X)
    await_raw(Z2, B)
    send_raw(Z2, B, XP, Z2X)
    normalize(Z2, A)
    normalize(Z2, B)
    multiply(ZM, True)
    multiply(ZP, True)
    multiply(Z2, False)
    multiply(Z2, True)
    await_raw(ZMX, A)
    normalize(ZMX, A)
    await_raw(ZPX, A)
    normalize(ZPX, A)
    await_raw(Z2X, A)
    normalize(Z2X, A)
    await_raw(ZMX, B)
    normalize(ZMX, B)
    await_raw(ZPX, B)
    normalize(ZPX, B)
    multiply(ZMX, False)
    await_raw(Z2X, B)
    normalize(Z2X, B)
    multiply(ZPX, False)
    multiply(Z2X, False)
    multiply(ZMX, True)
    multiply(ZPX, True)
    multiply(Z2X, True)
    for cp in stat_copies + list(sends.values()) + list(d_copies.values()):
        cp.wait_send()


def head_norm_phase(acc, gains, outs, qstat, qsend, qrecv, meanwhile):
    half = acc.shape[1]
    wq = outs[0].shape[1]
    for side in range(2):
        for i in range(2):
            values = acc[side, :, i * wq:(i + 1) * wq]
            qstat[0, 2 * side + i:2 * side + i + 1] = lane_sums(values * values)
    copies = []
    for flip in (False, True):
        for role in range(8):
            if role == OWN and not flip:
                continue
            there = BACK[role] + 8 * flip
            copies.append(
                remote(qstat.at[0], qstat.at[there], qsend.at[role + 8 * flip], qrecv.at[there], hid_device(role, flip))
            )
    for side in range(2):
        outs[2][pl.ds(side * half, half)] = acc[side, :, 2 * wq:3 * wq].astype(BF16)
    meanwhile()
    for cp in copies:
        cp.wait_recv()
    sums = qstat[0]
    for i in range(1, 16):
        sums = sums + qstat[i]
    scales = lax.rsqrt(rows_to_columns(sums * (1.0 / (16 * wq)), 128) + EPS)
    for side in range(2):
        for i in range(2):
            at = (2 * side + i) * 128
            by = scales[:, at:at + 1] * (SCORE_SCALE if i == 0 else 1.0)
            outs[i][pl.ds(side * half, half)] = (acc[side, :, i * wq:(i + 1) * wq] * by * gains[i][...]).astype(BF16)
    for cp in copies:
        cp.wait_send()


def attend_phase(q_ref, k_ref, v_ref, clip_ref, out_ref, qb, kb, vb, crow, best, acc, obuf,
                 xsend, xrecv, ysend, yrecv, csend, crecv, osem):
    rows = q_ref.shape[0]
    tile = rows // 2
    xh = lax.rem(lax.axis_index("seq"), 2)
    mine = pl.ds(pl.multiple_of(xh * HEAD_DIM, HEAD_DIM), HEAD_DIM)
    other = pl.ds(pl.multiple_of((1 - xh) * HEAD_DIM, HEAD_DIM), HEAD_DIM)
    low = pl.ds(0, HEAD_DIM)
    peers = [(y, f) for y in range(4) for f in (0, 1) if (y, f) != (0, 0)]
    def to(src, dst, send_sem, recv_sem, y, f):
        return pltpu.make_async_remote_copy(
            src, dst, send_sem, recv_sem, device_id=seq_device(y, f), device_id_type=MESH
        )

    def clip_copy(y, f):
        there = Y_BACK[y] * 2 + f
        return to(crow.at[0], crow.at[there], csend.at[y * 2 + f], crecv.at[there], y, f)

    x_copies = {
        "k": lambda: to(k_ref.at[:, other], kb.at[1, :, low], xsend.at[0], xrecv.at[0], 0, 1),
        "v": lambda: to(v_ref.at[:, other], vb.at[1, :, low], xsend.at[1], xrecv.at[1], 0, 1),
        "q": lambda: to(q_ref.at[:, other], qb.at[pl.ds(rows, rows), low], xsend.at[2], xrecv.at[2], 0, 1),
    }

    routes = {
        ("k", 2): (0, 2), ("k", 4): (0, 1), ("k", 3): (1, 2), ("k", 5): (1, 1), ("k", 6): (2, 2), ("k", 7): (3, 2),
        ("v", 2): (0, 2), ("v", 4): (0, 1), ("v", 3): (1, 2), ("v", 5): (1, 1), ("v", 6): (4, 1), ("v", 7): (5, 1),
    }

    def y_copy(name, to_slot):
        slot, y_role = routes[name, to_slot]
        buf, which = (kb, 0) if name == "k" else (vb, 1)
        return to(
            buf.at[slot, :, low], buf.at[to_slot, :, low],
            ysend.at[which, to_slot], yrecv.at[which, to_slot], y_role, 0,
        )

    def send_clips():
        crow[0] = clip_ref[...]
        for y, f in peers:
            clip_copy(y, f).start()

    def send_values():
        vb[0, :, 0:HEAD_DIM] = v_ref[:, mine]
        y_copy("v", 4).start()
        y_copy("v", 2).start()
        x_copies["v"]().start()

    def send_keys():
        kb[0, :, 0:HEAD_DIM] = k_ref[:, mine]
        y_copy("k", 2).start()
        y_copy("k", 4).start()
        x_copies["k"]().start()

    def mark_keys(slot):
        kb[slot, :, HEAD_DIM:2 * HEAD_DIM] = jnp.where(clip_one_hot(crow[slot], HEAD_DIM, HEAD_DIM), 0.0, FAR).astype(BF16)

    def mark_queries(side):
        qb[pl.ds(pl.multiple_of(side * rows, rows), rows), HEAD_DIM:2 * HEAD_DIM] = (
            clip_one_hot(crow[side], HEAD_DIM, HEAD_DIM).astype(F32).astype(BF16)
        )

    def attend_pair(slot, side):
        ats = [pl.ds(pl.multiple_of(side * rows + i * tile, tile), tile) for i in range(2)]
        scores = [
            lax.dot_general(qb[at], kb[slot], (((1,), (1,)), ((), ())), preferred_element_type=F32) for at in ats
        ]
        olds = [best[at] for at in ats]
        before = [acc[at] for at in ats]
        done = []
        for i in range(2):
            old = olds[i][:, 0:1]
            fresh = jnp.maximum(old, jnp.max(scores[i], axis=1, keepdims=True))
            weights = jnp.exp2(scores[i] - fresh).astype(BF16)
            mixed = jnp.dot(weights, vb[slot], preferred_element_type=F32)
            done.append((fresh, before[i] * jnp.exp2(old - fresh) + mixed))
        for i in range(2):
            best[ats[i]] = jnp.broadcast_to(done[i][0], (tile, HEAD_DIM))
            acc[ats[i]] = done[i][1]

    def prepare():
        best[...] = jnp.full(best.shape, 3.0 * FAR, F32)
        acc[...] = jnp.zeros_like(acc)
        for y, f in peers:
            clip_copy(y, f).wait_recv()

        def mark_slot(slot, carry):
            mark_keys(slot)
            vb[slot, :, HEAD_DIM:2 * HEAD_DIM] = jnp.ones((rows, HEAD_DIM), BF16)
            return carry

        def mark_side(side, carry):
            mark_queries(side)
            return carry

        lax.fori_loop(0, 8, mark_slot, 0)
        lax.fori_loop(0, 2, mark_side, 0)

    def early(i, carry):
        @pl.when(i == 1)
        def _():
            x_copies["v"]().wait_recv()
            y_copy("v", 5).start()
            x_copies["k"]().wait_recv()
            y_copy("k", 3).start()
            x_copies["q"]().start()
            y_copy("k", 2).wait_recv()
            y_copy("v", 4).wait_recv()
            y_copy("k", 6).start()
            y_copy("v", 6).start()
            y_copy("v", 3).start()
            y_copy("k", 5).start()

        @pl.when(i == 2)
        def _():
            y_copy("v", 2).wait_recv()

        @pl.when(i == 3)
        def _():
            y_copy("k", 4).wait_recv()

        @pl.when(i == 4)
        def _():
            x_copies["q"]().wait_recv()

        j = lax.rem(i, 4)
        attend_pair(j + j // 3, i // 4)
        return carry

    def finished(side):
        at = pl.ds(side * rows, rows)
        return (acc[at, 0:HEAD_DIM] / acc[at, HEAD_DIM:2 * HEAD_DIM]).astype(BF16)

    def back():
        return to(obuf, out_ref.at[:, mine], osem.at[0], osem.at[1], 0, 1)

    def late(i, carry):
        @pl.when(i == 0)
        def _():
            y_copy("k", 3).wait_recv()
            y_copy("k", 7).start()
            y_copy("v", 5).wait_recv()
            y_copy("v", 7).start()
            y_copy("k", 6).wait_recv()
            y_copy("v", 6).wait_recv()

        @pl.when(i == 2)
        def _():
            y_copy("v", 3).wait_recv()

        @pl.when(i == 4)
        def _():
            y_copy("k", 5).wait_recv()

        @pl.when(i == 6)
        def _():
            y_copy("k", 7).wait_recv()
            y_copy("v", 7).wait_recv()

        @pl.when(i == 7)
        def _():
            obuf[...] = finished(1)
            back().start()

        p = i // 2
        attend_pair(6 - 3 * p + 5 * (p // 2) + 5 * (p // 3), lax.rem(i + p // 3, 2))
        return carry

    def run():
        qb[pl.ds(0, rows), 0:HEAD_DIM] = q_ref[:, mine]
        lax.fori_loop(0, 8, early, 0)
        lax.fori_loop(0, 8, late, 0)
        out_ref[:, mine] = finished(0)
        back().wait()
        for y, f in peers:
            clip_copy(y, f).wait_send()
        for name in x_copies:
            x_copies[name]().wait_send()
        for name, slot in routes:
            y_copy(name, slot).wait_send()

    return send_clips, prepare, send_values, send_keys, run


def scatter_phase(a_ref, w_copies, own, hot_ref, gate_ref, wbuf, terms, got, land, gate_buf,
                  dsend, drecv, nsend, nrecv):
    depth, full = wbuf.shape[1], wbuf.shape[2]
    half = got.shape[1]
    part = terms.at[0]
    quarter = half // 2
    core = hid_place()[2]
    d_copies = {}
    arrived = {}

    def multiply(role):
        w_copies[role].wait()

        def row_half(i, carry):
            side = lax.rem(core + i, 2)
            rows = pl.ds(pl.multiple_of(side * half, half), half)
            terms[i, role] = jnp.dot(a_ref[rows], wbuf[role], preferred_element_type=F32).astype(BF16)
            return carry

        row_half(1, 0)
        d_copies[role] = remote(
            terms.at[1, role], got.at[role], dsend.at[role], drecv.at[role], hid_device(OWN, True)
        )
        row_half(0, 0)

    def send(role, which, to_role, slot):
        rows = pl.ds(which * quarter, quarter)
        arrived[slot, which] = remote(
            part.at[role, rows], land.at[slot, rows], nsend.at[slot, which], nrecv.at[slot, which],
            hid_device(to_role, False),
        )

    def fold(role, which, slots=(), last=False):
        rows = pl.ds(which * quarter, quarter)
        for slot in slots:
            arrived[slot, which].wait_recv()

        def lane_tile(n, carry):
            here = pl.ds(pl.multiple_of(n * 128, 128), 128)
            value = part[role, rows, here].astype(F32) + got[role, rows, here].astype(F32)
            for slot in slots:
                value = value + land[slot, rows, here].astype(F32)
            if last:
                own[rows, here] = (own[rows, here].astype(F32) + gate_buf[rows, here] * value).astype(BF16)
            else:
                part[role, rows, here] = value.astype(BF16)
            return carry

        lax.fori_loop(0, full // 128, lane_tile, 0)

    multiply(Z2X)
    multiply(ZPX)
    d_copies[Z2X].wait_recv()
    fold(Z2X, A)
    send(Z2X, A, XP, 0)
    fold(Z2X, B)
    send(Z2X, B, XP, 0)
    multiply(ZMX)
    d_copies[ZPX].wait_recv()
    fold(ZPX, A)
    send(ZPX, A, ZP, 1)
    d_copies[ZMX].wait_recv()
    fold(ZMX, A)
    send(ZMX, A, ZM, 2)
    fold(ZPX, B)
    send(ZPX, B, ZP, 1)
    fold(ZMX, B)
    send(ZMX, B, ZM, 2)
    multiply(Z2)
    multiply(ZP)
    multiply(ZM)
    d_copies[Z2].wait_recv()
    fold(Z2, A, (0,))
    send(Z2, A, ZP, 3)
    multiply(XP)
    d_copies[ZP].wait_recv()
    fold(ZP, B)
    d_copies[ZM].wait_recv()
    fold(ZM, A)
    d_copies[XP].wait_recv()
    fold(XP, A, (1, 2))
    send(XP, A, XP, 7)
    fold(Z2, B, (0,))
    send(Z2, B, ZM, 4)
    send(ZP, B, ZP, 5)
    send(ZM, A, ZM, 6)
    multiply(OWN)
    fold(XP, B, (1, 2))
    send(XP, B, XP, 7)
    fold(ZP, A, (3,))
    send(ZP, A, ZP, 5)
    fold(ZM, B, (4,))
    send(ZM, B, ZM, 6)
    hot_rows = hot_ref[pl.ds(pl.multiple_of(core * half, half), half)]
    gate_buf[...] = jnp.dot(hot_rows, pieces(gate_ref[...], 3), preferred_element_type=F32)
    d_copies[OWN].wait_recv()
    fold(OWN, A, (7, 6, 5), True)
    fold(OWN, B, (7, 5, 6), True)
    for cp in list(arrived.values()) + list(d_copies.values()):
        cp.wait_send()


def unpair_rows(own, result, theirs, fsem):
    half, full = own.shape
    part = full // 2
    core = hid_place()[2]
    rows = pl.ds(core * half, half)
    values = own[...].astype(F32)
    turned = pltpu.roll(values, part, 1)
    theirs[...] = jnp.where(core == 0, turned, values)[:, 0:part].astype(BF16)
    back = remote(theirs, result.at[rows], fsem.at[0], fsem.at[1], hid_device(OWN, True))
    result[rows] = jnp.where(core == 0, values, turned)[:, 0:part].astype(BF16)
    back.wait()


GATHER_SEMS = [(8,), (8,), (8, 2), (8, 2), (8, 2), (8, 2)]
ATTEND_SEMS = [(3,), (3,), (2, 8), (2, 8), (8,), (8,), (2,)]
SCATTER_SEMS = [(8,), (8,), (8, 2), (8, 2)]


def sems(shapes):
    return [pltpu.SemaphoreType.DMA(s) for s in shapes]


def gather_scratch(half, full, width):
    return [
        pltpu.VMEM((8, half, full), BF16),
        pltpu.VMEM((2, 8, half, full), BF16),
        pltpu.VMEM((8, 2, half), F32),
        pltpu.VMEM((2, half, 128), F32),
        pltpu.VMEM((8, full, width), BF16),
        pltpu.VMEM((2, half, width), F32),
    ]


def attend_scratch(rows):
    return [
        pltpu.VMEM((2 * rows, 2 * HEAD_DIM), BF16),
        pltpu.VMEM((8, rows, 2 * HEAD_DIM), BF16),
        pltpu.VMEM((8, rows, 2 * HEAD_DIM), BF16),
        pltpu.VMEM((8, 1, rows), F32),
        pltpu.VMEM((2 * rows, HEAD_DIM), F32),
        pltpu.VMEM((2 * rows, 2 * HEAD_DIM), F32),
        pltpu.VMEM((rows, HEAD_DIM), BF16),
    ]


def scatter_scratch(half, full):
    return [pltpu.VMEM((8, half, full), BF16), pltpu.VMEM((8, half, full), BF16), pltpu.VMEM((half, full), F32)]


def block_kernel(tokens, clip_ids, clip_step, table, w_query, w_key, w_value, q_gain, k_gain, w_out, w_up, w_down, out_ref,
                 x_turned, clip_ref, mods, gates, x, pair, hot, q, k, v, attended, hidden, qstat, w_first, w_mix,
                 w_last, acc, *refs):
    (x_sem, t_sem, p_sem, w_sem, up_sem, mix_sem, last_sem, qs_sem, qr_sem, free), refs = refs[:10], refs[10:]
    gather_bufs, refs = refs[:4], refs[4:]
    attend_bufs, refs = refs[:7], refs[7:]
    raw = gather_bufs[0]
    scatter_bufs, refs = (gather_bufs[1],) + refs[:3], refs[3:]
    gather_sems, attend_sems, scatter_sems = refs[:6], refs[6:13], refs[13:]
    half = acc.shape[1]
    width = w_query.shape[1]
    wide = w_up.shape[1]

    part, full = x.shape[1], w_last.shape[2]
    x_copy = pltpu.make_async_copy(tokens, x_turned, x_sem.at[0])
    x_copy.start()
    everyone_here = greet(True, True, True)
    t_copies = [
        pltpu.make_async_copy(table.at[c], mods.at[i], t_sem.at[i]) for i, c in enumerate((0, 1, 3, 4))
    ] + [
        pltpu.make_async_copy(
            table.at[c, :, pl.ds(pl.multiple_of(chip_of(OWN) * full, 128), full)], gates.at[i], t_sem.at[4 + i]
        )
        for i, c in enumerate((2, 5))
    ]
    for cp in t_copies:
        cp.start()
    first = load_columns_of_rows((w_query, w_key, w_value), w_first, w_sem, (width,) * 3)
    clip_ref[...] = clip_ids[...].astype(F32).reshape(clip_ref.shape)
    clip_hot = clip_one_hot(clip_ref[...], 8, 8).astype(F32).astype(BF16)
    steps = lax.dot_general(
        clip_step[...].astype(F32).astype(BF16), jnp.ones((1, hot.shape[1]), BF16), (((0,), (0,)), ((), ())),
        preferred_element_type=F32,
    )
    lane = lax.rem(lax.broadcasted_iota(jnp.int32, steps.shape, 1), hot.shape[1] // 3).astype(F32)
    step_hot = (steps == lane).astype(F32).astype(BF16)
    hot[...] = jnp.dot(clip_hot, step_hot, preferred_element_type=F32).astype(BF16)
    x_copy.wait()
    x[...] = lax.dot_general(
        x_turned[...], identity(part), (((0,), (0,)), ((), ())), preferred_element_type=F32
    ).astype(BF16)
    everyone_here()
    send_clips, prepare, send_values, send_keys, attend = attend_phase(
        q, k, v, clip_ref, attended, *attend_bufs, *attend_sems
    )
    pair_rows(x, raw, pair, p_sem)
    send_clips()
    for cp in t_copies:
        cp.wait()
    mix = load_blocks_of_columns(w_out, w_mix, mix_sem)
    last = load_blocks_of_columns(w_down, w_last, last_sem)
    gather_phase(hot, mods, 1, first, 3, 3 * width, *gather_bufs, w_first, acc, *gather_sems, meanwhile=prepare)
    head_norm_phase(acc, (q_gain, k_gain), (q, k, v), qstat, qs_sem, qr_sem, send_values)
    send_keys()
    attend()
    up = load_columns_of_rows((w_up,), w_first, up_sem, (wide,))
    scatter_phase(attended, mix, raw.at[OWN], hot, gates.at[0], w_mix, *scatter_bufs, *scatter_sems)
    pl.semaphore_signal(free, inc=1, device_id=hid_device(OWN, True), device_id_type=MESH)
    gather_phase(hot, mods, 3, up, 1, wide, *gather_bufs, w_first, acc, *gather_sems, free=free)
    for side in range(2):
        hidden[pl.ds(side * half, half)] = jax.nn.gelu(acc[side, :, 0:wide], approximate=True).astype(BF16)
    scatter_phase(hidden, last, raw.at[OWN], hot, gates.at[1], w_last, *scatter_bufs, *scatter_sems)
    unpair_rows(raw.at[OWN], x, pair, p_sem)
    out_ref[...] = lax.dot_general(
        identity(part), x[...], (((1,), (1,)), ((), ())), preferred_element_type=F32
    ).astype(BF16)


def block(tokens_turned, clip_id, clip_step, table, w_query, w_key, w_value, q_gain, k_gain, w_out, w_up, w_down):
    part, rows = tokens_turned.shape
    steps = table.shape[1]
    half, full = rows // 2, 2 * part
    width, wide = w_query.shape[1], w_up.shape[1]
    gather = gather_scratch(half, full, 3 * width)
    scratch = [
        pltpu.VMEM((part, rows), BF16),
        pltpu.VMEM((1, rows), F32),
        pltpu.VMEM((4, steps, table.shape[2]), F32),
        pltpu.VMEM((2, steps, full), F32),
        pltpu.VMEM((rows, part), BF16),
        pltpu.VMEM((half, part), BF16),
        pltpu.VMEM((rows, 3 * steps), BF16),
        pltpu.VMEM((rows, width), BF16),
        pltpu.VMEM((rows, width), BF16),
        pltpu.VMEM((rows, width), BF16),
        pltpu.VMEM((rows, width), BF16),
        pltpu.VMEM((rows, wide), BF16),
        pltpu.VMEM((16, 4, half), F32),
        gather[4],
        pltpu.VMEM((8, width, full), BF16),
        pltpu.VMEM((8, wide, full), BF16),
        gather[5],
    ]
    scratch += sems([(1,), (6,), (2,), (8, 3), (8, 1), (8,), (8,), (16,), (16,)])
    scratch += [pltpu.SemaphoreType.REGULAR]
    scratch += gather[:4] + attend_scratch(rows) + scatter_scratch(half, full)
    scratch += sems(GATHER_SEMS + ATTEND_SEMS + SCATTER_SEMS)
    return pl.pallas_call(
        block_kernel,
        out_shape=jax.ShapeDtypeStruct((part, rows), BF16),
        in_specs=[ANYSPEC, VSPEC, VSPEC, ANYSPEC, ANYSPEC, ANYSPEC, ANYSPEC, VSPEC, VSPEC, ANYSPEC, ANYSPEC, ANYSPEC],
        out_specs=VSPEC,
        scratch_shapes=scratch,
        compiler_params=pltpu.CompilerParams(collective_id=1, has_side_effects=True, vmem_limit_bytes=60 << 20),
        name="block",
    )(tokens_turned, clip_id, clip_step, table, w_query, w_key, w_value, q_gain, k_gain, w_out, w_up, w_down)


def shards(tokens, clip_id, clip_step, mod_table, w_query, w_key, w_value, q_gain, k_gain, w_out, w_up, w_down):
    return block(
        tokens.T, clip_id, clip_step[None, :], mod_table.transpose(1, 0, 2), w_query, w_key, w_value,
        q_gain[None, :], k_gain[None, :], w_out, w_up, w_down,
    ).T


def solution(mesh):
    placed = (
        P("seq", "hid"), P("seq"), P(), P(), P(None, "hid"), P(None, "hid"), P(None, "hid"), P("hid"), P("hid"),
        P("hid", None), P(None, "hid"), P("hid", None),
    )
    return jax.shard_map(shards, mesh=mesh, in_specs=placed, out_specs=P("seq", "hid"), check_vma=False)
```
